32 devices in a mesh: dp: 4 (over z), expert: 8 (over y, x, core).
Axes of the slice: x: 2, y: 2, z: 4, core: 2. Of those that a mesh axis runs over, the one named last changes fastest.
Arguments:
- block_input: bfloat16 [12608, 768], P(('dp', 'expert')), may hold values from -6 to 6
- out_grad: bfloat16 [12608, 768], P(('dp', 'expert')), may hold values from -6 to 6
- expert_ids: int32 [12608, 2], P(('dp', 'expert')), may hold values from 0 to 7, all different within a row
- slot_order: int32 [32, 394], P(('dp', 'expert')), may hold values from 0 to 393, each once within a row
- joint_weight: bfloat16 [768, 2304], P('expert'), may hold values from -0.21875 to 0.21875
- out_weight: bfloat16 [768, 768], P('expert'), may hold values from -0.625 to 0.625
- router_weight: bfloat16 [768, 8], P('expert'), may hold values from -0.4375 to 0.4375
- norm_gains: bfloat16 [2, 768], P(None, 'expert'), may hold values from 0.099609375 to 1.8984375
- norm_shifts: bfloat16 [2, 768], P(None, 'expert'), may hold values from -3 to 3
- attention_bias: bfloat16 [3, 768], P(None, 'expert'), may hold values from -3 to 3
- up_weight: bfloat16 [8, 768, 3072], P('expert'), may hold values from -0.21875 to 0.21875
- down_weight: bfloat16 [8, 3072, 768], P('expert'), may hold values from -3.5 to 3.5
- up_bias: bfloat16 [8, 3072], P('expert'), may hold values from -3 to 3
- down_bias: bfloat16 [8, 768], P('expert'), may hold values from -4 to 4
Outputs:
- block_output: bfloat16 [12608, 768], P(('dp', 'expert'))
- input_grad: bfloat16 [12608, 768], P(('dp', 'expert'))
- joint_grad: float32 [768, 2304], P('expert')
- out_weight_grad: float32 [768, 768], P('expert')
- router_grad: float32 [768, 8], P('expert')
- gains_grad: float32 [2, 768], P(None, 'expert')
- shifts_grad: float32 [2, 768], P(None, 'expert')
- attention_bias_grad: float32 [3, 768], P(None, 'expert')
- up_grad: float32 [8, 768, 3072], P('expert', None, 'dp')
- down_grad: float32 [8, 3072, 768], P('expert', 'dp')
- up_bias_grad: float32 [8, 3072], P('expert', 'dp')
- down_bias_grad: float32 [8, 768], P('expert', 'dp')
The draws below stay inside these ranges and needn't reach their ends.
Inputs may be any that keep to these rules, and one draw needn't show every extreme that they name: `expert_ids`: the two experts of a token differ. `slot_order`: each row is a permutation of the 394 token positions of one device.
All inputs are finite; a program needn't handle non-finite values.
Results may differ from the reference program's by a relative error of at most 0.024.
Values may be sent and summed in bfloat16 or wider, within the bound.
No kernel may reach another device: no remote copies, remote signals or barrier semaphores. Data moves between devices by JAX's collectives and lax.ppermute only.
A program may use at most 192 MiB of HBM per device.

```python
import jax
import jax.numpy as jnp
from jax import lax

D = 768
HEADS = 12
HEAD_DIM = 64
FF = 3072
SEQ = 197
IMG_DEV = 2
EXPERTS = 8
TOK_DEV = 394
TOKENS = 12608
CAP = 124
N_DP = 4
N_EXPERT = 8


def level_of(rng, dims, cuts, smallest, largest):
    level = 1.0
    for position, parts in cuts:
        heights = jax.random.uniform(jax.random.fold_in(jax.random.fold_in(rng, 6), position), (parts,), jnp.float32, smallest / len(cuts), largest / len(cuts))
        level = level * jnp.repeat(jnp.exp(heights), dims[position] // parts).reshape((-1,) + (1,) * (len(dims) - 1 - position))
    return level


def choose_distinct(stream_key, rows, count, top, lift):
    order = jax.random.permutation(jax.random.fold_in(stream_key, 1), count)
    favour = order
    for power in range(3):
        favour = favour * favour // count
    favour = favour * lift // count
    chance = jax.random.randint(jax.random.fold_in(stream_key, 2), (rows, count), 0, 4096) + favour
    sure = jax.random.permutation(jax.random.fold_in(stream_key, 3), rows)[jnp.arange(count) % rows]
    chance = jnp.where(jnp.arange(rows)[:, None] == sure[None, :], 1 << 14, chance)
    merit = chance * count + jnp.arange(count)
    return lax.top_k(merit.astype(jnp.int32), top)[1].astype(jnp.int32)


def noise(stream_key, shape, deviation, reach, pieces=(), kind=jnp.bfloat16):
    values = jax.random.normal(stream_key, shape, jnp.float32) * deviation
    if len(pieces) > 0:
        values = level_of(stream_key, shape, pieces, -0.22, 0.18) * values
    return jnp.clip(values, min=-reach, max=reach).astype(kind)


def setup_inputs(seed: int = 0) -> dict:
    seeds = jax.random.split(jax.random.key(seed), 15)
    return {
        "block_input": noise(seeds[0], (TOKENS, D), 1.0, 6.0, ((0, 32),)),
        "out_grad": noise(seeds[1], (TOKENS, D), 1.0, 6.0, ((0, 32),)),
        "expert_ids": choose_distinct(seeds[2], TOKENS, EXPERTS, 2, 2048),
        "slot_order": jax.vmap(lambda own: jax.random.permutation(own, TOK_DEV))(jax.random.split(seeds[3], (N_DP * N_EXPERT))).reshape((N_DP * N_EXPERT, TOK_DEV)).astype(jnp.int32),
        "joint_weight": noise(seeds[4], (D, 3 * D), D ** -0.5, 0.21875, ((0, 8),)),
        "out_weight": noise(seeds[5], (D, D), (D // 8) ** -0.5, 0.625, ((0, 8),)),
        "router_weight": noise(seeds[6], (D, EXPERTS), (D // 4) ** -0.5, 0.4375, ((0, 8),)),
        "norm_gains": jnp.clip(1.0 + 0.18 * jax.random.normal(seeds[7], (2, D), jnp.float32), 0.099609375, 1.8984375).astype(jnp.bfloat16),
        "norm_shifts": noise(seeds[8], (2, D), 0.5, 3.0, ((1, 8),)),
        "attention_bias": noise(seeds[9], (3, D), 0.5, 3.0, ((1, 8),)),
        "up_weight": noise(seeds[10], (EXPERTS, D, FF), D ** -0.5, 0.21875, ((0, 8),)),
        "down_weight": noise(seeds[11], (EXPERTS, FF, D), (max(1, FF // 1024)) ** -0.5, 3.5, ((0, 8),)),
        "up_bias": noise(seeds[12], (EXPERTS, FF), 0.5, 3.0, ((0, 8),)),
        "down_bias": noise(seeds[13], (EXPERTS, D), 1.0, 4.0, ((0, 8),)),
    }


@jax.custom_vjp
def low(v):
    return lax.optimization_barrier(v.astype(jnp.bfloat16)).astype(jnp.float32)

@jax.custom_vjp
def low_back(v):
    return v

def low_keep(v):
    return (low(v), None)

def low_pass(kept, grad):
    return (grad,)

def back_keep(v):
    return (v, None)

def back_low(kept, grad):
    return (low(grad),)
low.defvjp(low_keep, low_pass)
low_back.defvjp(back_keep, back_low)
norm_eps = 1e-06
full_precision = lax.Precision.HIGHEST

def layer_norm(values, gain_row, shift_row):
    row_mean = lax.optimization_barrier(jnp.mean(values, axis=-1, keepdims=True))
    centered = values - row_mean
    row_var = lax.optimization_barrier(jnp.mean(centered * centered, axis=-1, keepdims=True))
    return centered * lax.rsqrt(row_var + norm_eps) * gain_row + shift_row

def gelu_tanh(values):
    return jax.nn.gelu(values, approximate=True)

def matmul_high(left, right):
    return jnp.dot(left, right, precision=full_precision)

def slot_table(route_rows, order_row, expert_count, capacity):
    tokens_here = route_rows.shape[0]
    ordered = jnp.take(route_rows, order_row, axis=0)
    expert_iota = jnp.arange(expert_count, dtype=jnp.int32)
    first_hot = (ordered[:, 0:1] == expert_iota[None, :]).astype(jnp.int32)
    second_hot = (ordered[:, 1:2] == expert_iota[None, :]).astype(jnp.int32)
    first_slot = lax.optimization_barrier(jnp.sum((jnp.cumsum(first_hot, axis=0) - first_hot) * first_hot, axis=1)).astype(jnp.int32)
    second_base = lax.optimization_barrier(jnp.sum(first_hot, axis=0, keepdims=True)).astype(jnp.int32)
    second_slot = lax.optimization_barrier(jnp.sum((jnp.cumsum(second_hot, axis=0) - second_hot + second_base) * second_hot, axis=1)).astype(jnp.int32)
    slot_rank = jnp.stack([first_slot, second_slot], axis=1).astype(jnp.int32)
    flat_rank = jnp.where(slot_rank < capacity, ordered * capacity + slot_rank, expert_count * capacity).astype(jnp.int32)
    token_flat = jnp.zeros((tokens_here, 2), jnp.int32).at[order_row].set(flat_rank)
    token_index = jnp.broadcast_to(jnp.arange(tokens_here, dtype=jnp.int32)[:, None], (tokens_here, 2))
    source = jnp.full((expert_count * capacity,), tokens_here, jnp.int32).at[token_flat.reshape(-1)].set(token_index.reshape(-1), mode='drop')
    return (token_flat, source)

def block_forward(input_rows, route_rows, order_row, params):
    joint_weight, out_weight, router_weight, norm_gains, norm_shifts, attention_bias, up_weight, down_weight, up_bias, down_bias = params
    normed = low(layer_norm(input_rows, norm_gains[0], norm_shifts[0]))
    joint_bias = jnp.concatenate([attention_bias[0], jnp.zeros_like(attention_bias[0]), attention_bias[1]])
    projected = low_back(low(matmul_high(normed, joint_weight) + joint_bias))
    projected = projected.reshape(IMG_DEV, SEQ, 3, HEADS, HEAD_DIM)
    scores = low_back(jnp.einsum('ishd,ithd->ihst', projected[:, :, 0], projected[:, :, 1], precision=full_precision) * HEAD_DIM ** (-0.5))
    weighting = low(jax.nn.softmax(scores, axis=-1))
    attended = jnp.einsum('ihst,ithd->ishd', weighting, projected[:, :, 2], precision=full_precision).reshape(TOK_DEV, D)
    attended = low_back(low(attended))
    residual = input_rows + low_back(matmul_high(attended, out_weight)) + attention_bias[2]
    normed_two = low(layer_norm(residual, norm_gains[1], norm_shifts[1]))
    logits = low_back(matmul_high(normed_two, router_weight))
    gate_weights = jax.nn.softmax(logits, axis=-1)
    chosen = jnp.take_along_axis(gate_weights, route_rows, axis=1)
    token_flat, source = slot_table(route_rows, order_row, EXPERTS, CAP)
    dispatched = low_back(jnp.take(normed_two, source, axis=0, mode='fill', fill_value=0.0)).reshape(EXPERTS, CAP, D)
    pre_gelu = low_back(jnp.einsum('ecd,edf->ecf', dispatched, up_weight, precision=full_precision) + up_bias[:, None, :])
    hidden = low(gelu_tanh(pre_gelu))
    expert_out = jnp.einsum('ecf,efd->ecd', hidden, down_weight, precision=full_precision) + down_bias[:, None, :]
    expert_out = low_back(low(expert_out)).reshape(EXPERTS * CAP, D)
    picked = jnp.take(expert_out, token_flat, axis=0, mode='fill', fill_value=0.0)
    return residual + lax.optimization_barrier(jnp.sum(chosen[:, :, None] * picked, axis=1))

def reference(block_input, out_grad, expert_ids, slot_order, joint_weight, out_weight, router_weight, norm_gains, norm_shifts, attention_bias, up_weight, down_weight, up_bias, down_bias):
    params = tuple((member.astype(jnp.float32) for member in (joint_weight, out_weight, router_weight, norm_gains, norm_shifts, attention_bias, up_weight, down_weight, up_bias, down_bias)))
    block_count = N_DP * N_EXPERT
    blocked_routes = expert_ids.reshape(block_count, TOK_DEV, 2)
    checked = jax.checkpoint(block_forward)

    def whole_layer(input_all, weights):

        def one_block(dropped_carry, inputs):
            return (dropped_carry, checked(inputs[0], inputs[1], inputs[2], weights))
        _, produced = lax.scan(one_block, None, (input_all.reshape(block_count, TOK_DEV, D), blocked_routes, slot_order))
        return produced.reshape(TOKENS, D)
    output_value, pullback = jax.vjp(whole_layer, block_input.astype(jnp.float32), params)
    input_grad, param_grads = pullback(out_grad.astype(jnp.float32))
    joint_grad, out_weight_grad, router_grad, gains_grad, shifts_grad, attention_bias_grad, up_grad, down_grad, up_bias_grad, down_bias_grad = param_grads
    return (output_value.astype(jnp.bfloat16), input_grad.astype(jnp.bfloat16), joint_grad, out_weight_grad, router_grad, gains_grad, shifts_grad, attention_bias_grad, up_grad, down_grad, up_bias_grad, down_bias_grad)
```

```python
import jax
import jax.numpy as jnp
from jax import lax
from jax.sharding import PartitionSpec as P

HEADS = 12
HEAD_DIM = 64
SEQ = 197
LANES = 128
norm_eps = 1e-06


f32 = jnp.float32
bf16 = jnp.bfloat16


def round_up(value, step):
    return (value + step - 1) // step * step


def dot(left, right, dims):
    return lax.dot_general(left, right, (dims, ((), ())), preferred_element_type=f32)


def swap(value, axis, size, offset):
    return lax.ppermute(value, axis, [(i, i ^ offset) for i in range(size)])


def exchange(chunks, axis, size):
    return [chunks[0]] + [swap(chunks[d], axis, size, d) for d in range(1, size)]


def gather_rows(shard, axis, size):
    index = lax.axis_index(axis)
    same = [shard] + [swap(shard, axis, size, d) for d in range(2, size, 2)]
    other = [swap(part, axis, size, 1) for part in same]
    rows = shard.shape[0]
    whole = jnp.zeros((size * rows, shard.shape[1]), shard.dtype)
    for d in range(size):
        part = (same, other)[d % 2][d // 2]
        whole = lax.dynamic_update_slice(whole, part, ((index ^ d) * rows, 0))
    return whole


def normalise(values):
    row_mean = jnp.mean(values, axis=-1, keepdims=True)
    centered = values - row_mean
    row_var = jnp.mean(centered * centered, axis=-1, keepdims=True)
    scale = lax.rsqrt(row_var + norm_eps)
    return centered * scale, scale


def normalise_back(grads, hat, scale, gain):
    u = grads * gain
    return scale * (
        u
        - jnp.mean(u, axis=-1, keepdims=True)
        - hat * jnp.mean(u * hat, axis=-1, keepdims=True)
    )


def gelu_tanh(values):
    return jax.nn.gelu(values, approximate=True)


def slot_index(ids, order, experts, capacity, stride, index):
    tokens = ids.shape[0]
    place = jnp.arange(tokens, dtype=jnp.int32)
    hits = order[:, None] == place[None, :]
    position = jnp.sum(jnp.where(hits, place[:, None], 0), axis=0)
    position_row = jnp.sum(jnp.where(hits.T, place[None, :], 0), axis=1)
    earlier = (position_row[None, :] < position[:, None]).astype(bf16)
    expert_iota = jnp.arange(experts, dtype=jnp.int32)
    hot = [(ids[:, k : k + 1] == expert_iota[None, :]) for k in range(2)]
    counts = dot(
        earlier, jnp.concatenate(hot, axis=1).astype(bf16), ((1,), (0,))
    )
    base = jnp.sum(hot[0].astype(f32), axis=0, keepdims=True)
    first = jnp.sum(jnp.where(hot[0], counts[:, :experts], 0.0), axis=1)
    second = jnp.sum(jnp.where(hot[1], counts[:, experts:] + base, 0.0), axis=1)
    rank = jnp.stack([first, second], axis=1).astype(jnp.int32)
    return jnp.where(rank < capacity, (ids ^ index) * stride + rank, experts * stride)


def per_device(
    block_input,
    out_grad,
    expert_ids,
    slot_order,
    joint_weight,
    out_weight,
    router_weight,
    norm_gains,
    norm_shifts,
    attention_bias,
    up_weight,
    down_weight,
    up_bias,
    down_bias,
    *,
    expert_size,
    dp_size,
):
    index = lax.axis_index("expert")
    row_count, features = block_input.shape
    images = row_count // SEQ
    experts = router_weight.shape[1]
    capacity = max(2, (5 * row_count + 2 * experts - 1) // (2 * experts))
    stride = round_up(capacity + 1, 16)
    slots = experts * stride
    padded = round_up(SEQ, 16)
    tokens = images * padded
    hidden_units = up_weight.shape[2]
    head_scale = HEAD_DIM ** (-0.5)

    def pad_rows(values, fill=0):
        split = values.reshape(images, SEQ, values.shape[-1])
        return jnp.pad(
            split, ((0, 0), (0, padded - SEQ), (0, 0)), constant_values=fill
        ).reshape(tokens, values.shape[-1])

    def crop_rows(values):
        return values.reshape(images, padded, -1)[:, :SEQ].reshape(row_count, -1)

    small = jnp.concatenate(
        [router_weight, norm_gains.T, norm_shifts.T, attention_bias.T], axis=1
    )
    small_width = small.shape[1]
    small = jnp.pad(small, ((0, 0), (0, round_up(small_width, LANES) - small_width)))
    joint_cols = joint_weight.shape[1]
    first = gather_rows(jnp.concatenate([joint_weight, small], axis=1), "expert", expert_size)
    joint_full = first[:, :joint_cols]
    small_full = first[:, joint_cols:]
    out_shard, first_done = lax.optimization_barrier((out_weight, first[0, 0]))
    out_full = gather_rows(out_shard, "expert", expert_size)
    router_full = small_full[:, :experts]
    rows = small_full[:, experts:small_width].T.astype(f32)
    gains, shifts, biases = rows[0:2], rows[2:4], rows[4:7]

    flat = pad_rows(
        slot_index(expert_ids, slot_order[0], experts, capacity, stride, index),
        slots,
    )
    ids = pad_rows(expert_ids)
    slot_iota = jnp.arange(slots, dtype=jnp.int32)
    pick = [(flat[:, k : k + 1] == slot_iota[None, :]) for k in range(2)]
    pick_low = [member.astype(bf16) for member in pick]
    pick_both = (pick[0] | pick[1]).astype(bf16)
    grad_low = pad_rows(out_grad)
    grad_float = grad_low.astype(f32)
    grad_slots = dot(pick_both, grad_low, ((0,), (0,))).astype(bf16)
    grad_slots, first_done = lax.optimization_barrier((grad_slots, first_done))
    grad_slots = grad_slots.reshape(experts, stride, features)
    grad_arrived = exchange([grad_slots[d] for d in range(experts)], "expert", expert_size)

    input_low = pad_rows(block_input)
    input_float = input_low.astype(f32)
    hat_one, scale_one = normalise(input_float)
    normed_low = (hat_one * gains[0] + shifts[0]).astype(bf16)
    joint_bias = jnp.concatenate([biases[0], jnp.zeros_like(biases[0]), biases[1]])
    projected = (dot(normed_low, joint_full, ((1,), (0,))) + joint_bias).astype(bf16)
    heads = projected.reshape(images, padded, 3, HEADS, HEAD_DIM)
    query, key, value = heads[:, :, 0], heads[:, :, 1], heads[:, :, 2]
    scores = (
        jnp.einsum("ishd,ithd->ihst", query, key, preferred_element_type=f32) * head_scale
    )
    valid = jnp.arange(padded) < SEQ
    scores = jnp.where(valid, scores, -1e30)
    weighting = jax.nn.softmax(scores, axis=-1)
    weighting_low = weighting.astype(bf16)
    attended = jnp.einsum("ihst,ithd->ishd", weighting_low, value, preferred_element_type=f32)
    attended_low = attended.reshape(tokens, features).astype(bf16)
    residual = input_float + dot(attended_low, out_full, ((1,), (0,))) + biases[2]
    hat_two, scale_two = normalise(residual)
    two_low = (hat_two * gains[1] + shifts[1]).astype(bf16)
    logits = dot(two_low, router_full, ((1,), (0,)))
    gate_weights = jax.nn.softmax(logits, axis=-1)
    expert_iota = jnp.arange(experts, dtype=jnp.int32)
    choice = [(ids[:, k : k + 1] == expert_iota[None, :]) for k in range(2)]
    chosen = [
        jnp.sum(jnp.where(choice[k], gate_weights, 0.0), axis=1, keepdims=True)
        for k in range(2)
    ]

    dispatched = dot(pick_both, two_low, ((0,), (0,))).astype(bf16)
    dispatched = dispatched.reshape(experts, stride, features)
    slot_gate = jnp.sum(
        jnp.where(pick[0], chosen[0], 0.0) + jnp.where(pick[1], chosen[1], 0.0), axis=0
    ).reshape(experts, stride)
    gate_high = slot_gate.astype(bf16)
    rest = slot_gate - gate_high.astype(f32)
    gate_mid = rest.astype(bf16)
    gate_low = (rest - gate_mid.astype(f32)).astype(bf16)
    gate_row = jnp.concatenate(
        [jnp.pad(part, ((0, 0), (0, LANES - stride))) for part in (gate_high, gate_mid, gate_low)],
        axis=1,
    )
    gate_row = jnp.pad(gate_row, ((0, 0), (0, features - 3 * LANES)))
    spare = (jnp.arange(stride) == capacity)[None, :, None]
    dispatched = jnp.where(spare, gate_row[:, None, :], dispatched)
    arrived_list = exchange([dispatched[d] for d in range(experts)], "expert", expert_size)
    arrived = jnp.concatenate(arrived_list, axis=0)
    gate_parts = jnp.stack([part[capacity] for part in arrived_list]).astype(f32)
    gate_here = (
        gate_parts[:, :stride]
        + gate_parts[:, LANES : LANES + stride]
        + gate_parts[:, 2 * LANES : 2 * LANES + stride]
    )
    slot_grad = (
        gate_here.reshape(-1)[:, None] * jnp.concatenate(grad_arrived, axis=0).astype(f32)
    ).astype(bf16)

    up, down = up_weight[0], down_weight[0]
    pre_gelu = dot(arrived, up, ((1,), (0,))) + up_bias.astype(f32)
    hidden, gelu_back = jax.vjp(gelu_tanh, pre_gelu)
    hidden_low = hidden.astype(bf16)
    down_local = dot(hidden_low, slot_grad, ((0,), (0,))).astype(bf16)
    down_part = lax.psum_scatter(down_local, "dp", scatter_dimension=0, tiled=True)
    hidden_low, slot_grad, down_local = lax.optimization_barrier((hidden_low, slot_grad, down_local))
    expert_out = (dot(hidden_low, down, ((1,), (0,))) + down_bias.astype(f32)).astype(bf16)
    expert_out = expert_out.reshape(experts, stride, features)
    returned = jnp.concatenate(
        exchange([expert_out[d] for d in range(experts)], "expert", expert_size), axis=0
    )
    hidden_grad = dot(slot_grad, down, ((1,), (1,)))
    (inner_grad,) = gelu_back(hidden_grad)
    inner_low = inner_grad.astype(bf16)
    rows_grad = dot(inner_low, up, ((1,), (1,))).astype(bf16).reshape(experts, stride, features)
    rows_back = jnp.concatenate(
        exchange([rows_grad[d] for d in range(experts)], "expert", expert_size), axis=0
    )
    up_local = dot(arrived, inner_low, ((0,), (0,))).astype(bf16)
    up_part = lax.psum_scatter(up_local, "dp", scatter_dimension=1, tiled=True)
    bias_local = jnp.concatenate(
        [
            jnp.sum(inner_low, axis=0, dtype=f32).reshape(dp_size, -1),
            jnp.sum(slot_grad, axis=0, dtype=f32).reshape(dp_size, -1),
        ],
        axis=1,
    )
    dp_index = lax.axis_index("dp")
    bias_chunks = [
        lax.dynamic_index_in_dim(bias_local, dp_index ^ d, 0) for d in range(dp_size)
    ]
    bias_sum = sum(exchange(bias_chunks, "dp", dp_size))
    up_bias_grad = bias_sum[:, : hidden_units // dp_size]
    down_bias_grad = bias_sum[:, hidden_units // dp_size :]

    picked = [dot(pick_low[k], returned, ((1,), (0,))) for k in range(2)]
    block_output = crop_rows(
        (residual + chosen[0] * picked[0] + chosen[1] * picked[1]).astype(bf16)
    )
    gate_grad = [jnp.sum(grad_float * picked[k], axis=1, keepdims=True) for k in range(2)]
    mass_grad = sum(jnp.where(choice[k], gate_grad[k], 0.0) for k in range(2))
    logit_grad = (
        gate_weights * (mass_grad - jnp.sum(gate_weights * mass_grad, axis=1, keepdims=True))
    ).astype(bf16)
    router_local = dot(two_low, logit_grad, ((0,), (0,)))
    two_grad = dot(logit_grad, router_full, ((1,), (1,))) + dot(
        pick_both, rows_back, ((1,), (0,))
    )
    gain_two = jnp.sum(two_grad * hat_two, axis=0)
    shift_two = jnp.sum(two_grad, axis=0)
    residual_grad = grad_float + normalise_back(two_grad, hat_two, scale_two, gains[1])
    branch_low = residual_grad.astype(bf16)
    out_local = dot(attended_low, branch_low, ((0,), (0,)))
    attended_grad = dot(branch_low, out_full, ((1,), (1,))).astype(bf16)
    attended_grad = attended_grad.reshape(images, padded, HEADS, HEAD_DIM)

    weight_grad = jnp.einsum(
        "ishd,ithd->ihst", attended_grad, value, preferred_element_type=f32
    )
    value_grad = jnp.einsum(
        "ihst,ishd->ithd", weighting_low, attended_grad, preferred_element_type=f32
    )
    probs = weighting_low.astype(f32)
    score_grad = (
        probs * (weight_grad - jnp.sum(weight_grad * probs, axis=-1, keepdims=True))
    ).astype(bf16)
    query_grad = (
        jnp.einsum("ihst,ithd->ishd", score_grad, key, preferred_element_type=f32) * head_scale
    )
    key_grad = (
        jnp.einsum("ihst,ishd->ithd", score_grad, query, preferred_element_type=f32)
        * head_scale
    )
    projected_grad = (
        jnp.stack([query_grad, key_grad, value_grad], axis=2)
        .reshape(tokens, 3 * features)
        .astype(bf16)
    )
    joint_local = dot(normed_low, projected_grad, ((0,), (0,)))
    bias_sums = jnp.sum(projected_grad, axis=0, dtype=f32)
    normed_grad = dot(projected_grad, joint_full, ((1,), (1,)))
    gain_one = jnp.sum(normed_grad * hat_one, axis=0)
    shift_one = jnp.sum(normed_grad, axis=0)
    input_grad = crop_rows(
        (residual_grad + normalise_back(normed_grad, hat_one, scale_one, gains[0])).astype(bf16)
    )

    vectors = jnp.stack(
        [
            gain_one,
            gain_two,
            shift_one,
            shift_two,
            bias_sums[:features],
            bias_sums[2 * features :],
            jnp.sum(residual_grad, axis=0),
        ],
        axis=1,
    )
    packed = jnp.concatenate(
        [joint_local, out_local, router_local, vectors], axis=1
    ).astype(bf16)
    width = packed.shape[1]
    packed = jnp.pad(packed, ((0, 0), (0, round_up(width, LANES) - width)))
    shard_rows = features // expert_size
    packed = packed.reshape(expert_size, shard_rows, -1)
    blocks = [lax.dynamic_index_in_dim(packed, index ^ d, 0) for d in range(expert_size)]
    kept = jnp.concatenate(blocks[0::2], axis=0)
    sent = jnp.concatenate(blocks[1::2], axis=0)
    pair_sum = (kept.astype(f32) + swap(sent, "expert", expert_size, 1).astype(f32)).astype(bf16)
    parts = [pair_sum[0]] + [
        swap(pair_sum[d // 2], "expert", expert_size, d) for d in range(2, expert_size, 2)
    ]
    plane_sum = sum(part.astype(f32) for part in parts).astype(bf16)
    plane_sum = plane_sum.reshape(dp_size, shard_rows // dp_size, -1)
    dp_parts = exchange(
        [lax.dynamic_index_in_dim(plane_sum, dp_index ^ d, 0, keepdims=False) for d in range(dp_size)],
        "dp",
        dp_size,
    )
    dp_sum = sum(part.astype(f32) for part in dp_parts).astype(bf16)
    final = lax.all_gather(dp_sum, "dp", axis=0, tiled=True).astype(f32)
    ends = [joint_cols, joint_cols + features, joint_cols + features + experts]
    joint_grad = final[:, : ends[0]]
    out_weight_grad = final[:, ends[0] : ends[1]]
    router_grad = final[:, ends[1] : ends[2]]
    vector_grads = final[:, ends[2] : ends[2] + 7].T
    return (
        block_output,
        input_grad,
        joint_grad,
        out_weight_grad,
        router_grad,
        vector_grads[0:2],
        vector_grads[2:4],
        vector_grads[4:7],
        up_part[None].astype(f32),
        down_part[None].astype(f32),
        up_bias_grad,
        down_bias_grad,
    )


def solution(mesh):
    def body(*args):
        return per_device(
            *args, expert_size=mesh.shape["expert"], dp_size=mesh.shape["dp"]
        )

    in_specs = (
        P(("dp", "expert"), None),
        P(("dp", "expert"), None),
        P(("dp", "expert"), None),
        P(("dp", "expert"), None),
        P("expert", None),
        P("expert", None),
        P("expert", None),
        P(None, "expert"),
        P(None, "expert"),
        P(None, "expert"),
        P("expert", None, None),
        P("expert", None, None),
        P("expert", None),
        P("expert", None),
    )
    out_specs = (
        P(("dp", "expert"), None),
        P(("dp", "expert"), None),
        P("expert", None),
        P("expert", None),
        P("expert", None),
        P(None, "expert"),
        P(None, "expert"),
        P(None, "expert"),
        P("expert", None, "dp"),
        P("expert", "dp", None),
        P("expert", "dp"),
        P("expert", "dp"),
    )
    return jax.shard_map(
        body, mesh=mesh, in_specs=in_specs, out_specs=out_specs, check_vma=False
    )
```

```python
import functools

import jax
import jax.numpy as jnp
from jax import lax
from jax.experimental import pallas as pl
from jax.experimental.pallas import tpu as pltpu
from jax.sharding import PartitionSpec as P


HEADS = 12
HEAD_DIM = 64
SEQ = 197
LANES = 128
norm_eps = 1e-06


f32 = jnp.float32
bf16 = jnp.bfloat16
NN = ((1,), (0,))
NT = ((1,), (1,))
TN = ((0,), (0,))


def round_up(value, step):
    return (value + step - 1) // step * step


def dot(left, right, dims):
    return lax.dot_general(left, right, (dims, ((), ())), preferred_element_type=f32)


def swap(value, axis, size, offset):
    return lax.ppermute(value, axis, [(i, i ^ offset) for i in range(size)])


def exchange(chunks, axis, size):
    return [chunks[0]] + [swap(chunks[d], axis, size, d) for d in range(1, size)]


def gather_pieces(shard, axis, size):
    rows = shard.shape[0]
    if rows % 16:
        return [lax.all_gather(shard, axis, axis=0, tiled=True)], jnp.zeros((1,), jnp.int32)
    same = [shard] + [swap(shard, axis, size, d) for d in range(2, size, 2)]
    other = [swap(part, axis, size, 1) for part in same]
    pieces = [(same, other)[d % 2][d // 2] for d in range(size)]
    offsets = (lax.axis_index(axis) ^ jnp.arange(size, dtype=jnp.int32)) * rows
    return pieces, offsets


def normalise(values):
    row_mean = jnp.mean(values, axis=-1, keepdims=True)
    centered = values - row_mean
    row_var = jnp.mean(centered * centered, axis=-1, keepdims=True)
    scale = lax.rsqrt(row_var + norm_eps)
    return centered * scale, scale


def normalise_back(grads, hat, scale, gain):
    u = grads * gain
    return scale * (
        u
        - jnp.mean(u, axis=-1, keepdims=True)
        - hat * jnp.mean(u * hat, axis=-1, keepdims=True)
    )


def slot_index(ids, order, experts, capacity, stride, index):
    tokens = ids.shape[0]
    place = jnp.arange(tokens, dtype=jnp.int32)
    hits = order[:, None] == place[None, :]
    position = jnp.sum(jnp.where(hits, place[:, None], 0), axis=0)
    position_row = jnp.sum(jnp.where(hits.T, place[None, :], 0), axis=1)
    earlier = (position_row[None, :] < position[:, None]).astype(bf16)
    expert_iota = jnp.arange(experts, dtype=jnp.int32)
    hot = [(ids[:, k : k + 1] == expert_iota[None, :]) for k in range(2)]
    counts = dot(
        earlier, jnp.concatenate(hot, axis=1).astype(bf16), ((1,), (0,))
    )
    base = jnp.sum(hot[0].astype(f32), axis=0, keepdims=True)
    first = jnp.sum(jnp.where(hot[0], counts[:, :experts], 0.0), axis=1)
    second = jnp.sum(jnp.where(hot[1], counts[:, experts:] + base, 0.0), axis=1)
    rank = jnp.stack([first, second], axis=1).astype(jnp.int32)
    return jnp.where(rank < capacity, (ids ^ index) * stride + rank, experts * stride)


def shaped(shape, dtype):
    return jax.ShapeDtypeStruct(shape, dtype)


def full(shape):
    return pl.BlockSpec(shape, lambda *_: (0,) * len(shape))


def place(pieces, offsets_ref, out_ref):
    rows = pieces[0].shape[0]
    for k, piece in enumerate(pieces):
        out_ref[pl.ds(pl.multiple_of(offsets_ref[k], 16), rows), :] = piece[...]


def attend_kernel(experts, padded, offsets_ref, x_ref, *refs):
    pieces = refs[:-6]
    w_ref, par_ref, norm_ref, proj_ref, prob_ref, att_ref = refs[-6:]
    features = x_ref.shape[1]

    @pl.when(pl.program_id(0) == 0)
    def _():
        place(pieces, offsets_ref, w_ref)
        par = jnp.transpose(w_ref[:, 3 * features :].astype(f32))
        par_ref[...] = par[experts : experts + 8]

    hat, _ = normalise(x_ref[...].astype(f32))
    norm_ref[...] = (hat * par_ref[0:1] + par_ref[2:3]).astype(bf16)
    zero = jnp.zeros((1, features), f32)
    for third, bias in enumerate((par_ref[4:5], zero, par_ref[5:6])):
        cols = slice(third * features, (third + 1) * features)
        proj_ref[:, cols] = (dot(norm_ref[...], w_ref[:, cols], NN) + bias).astype(bf16)
    low = lax.broadcasted_iota(jnp.int32, (1, LANES), 1) < HEAD_DIM
    valid = lax.broadcasted_iota(jnp.int32, (1, padded), 1) < SEQ

    def pair(p, carry):
        def cols(third):
            return pl.ds(pl.multiple_of(third * features + p * LANES, LANES), LANES)

        query, key, value = (proj_ref[:, cols(third)] for third in range(3))
        outs = []
        for half in range(2):
            mine = low if half == 0 else ~low
            scores = dot(jnp.where(mine, query, jnp.zeros_like(query)), key, NT)
            scores = jnp.where(valid, scores * HEAD_DIM**-0.5, -1e30)
            powers = jnp.exp(scores - jnp.max(scores, axis=1, keepdims=True))
            probs = (powers / jnp.sum(powers, axis=1, keepdims=True)).astype(bf16)
            prob_ref[2 * p + half] = probs
            outs.append(dot(probs, value, NN))
        att_ref[:, cols(0)] = jnp.where(low, outs[0], outs[1]).astype(bf16)
        return carry

    lax.fori_loop(0, features // LANES, pair, 0, unroll=3)


def attend(x, pieces, offsets, experts, images):
    tokens, features = x.shape
    padded = tokens // images
    width = pieces[0].shape[1]
    image = lambda i, o: (i, 0)
    return pl.pallas_call(
        functools.partial(attend_kernel, experts, padded),
        grid_spec=pltpu.PrefetchScalarGridSpec(
            num_scalar_prefetch=1,
            grid=(images,),
            in_specs=[pl.BlockSpec((padded, features), image)]
            + [full(piece.shape) for piece in pieces],
            out_specs=[
                full((features, width)),
                full((8, features)),
                pl.BlockSpec((padded, features), image),
                pl.BlockSpec((padded, 3 * features), image),
                pl.BlockSpec((HEADS, padded, padded), lambda i, o: (i, 0, 0)),
                pl.BlockSpec((padded, features), image),
            ],
        ),
        out_shape=[
            shaped((features, width), bf16),
            shaped((8, features), f32),
            shaped((tokens, features), bf16),
            shaped((tokens, 3 * features), bf16),
            shaped((images * HEADS, padded, padded), bf16),
            shaped((tokens, features), bf16),
        ],
        cost_estimate=pl.CostEstimate(
            flops=12 * tokens * features * features, bytes_accessed=16 << 20, transcendentals=0
        ),
        name="attend",
    )(offsets, x, *pieces)


def hits_of(flat_ref, chunk, stride, k, width):
    lane = lax.broadcasted_iota(jnp.int32, (1, width), 1)
    wanted = jnp.where(lane < stride, lane + chunk * stride, -1)
    return flat_ref[:, k : k + 1] == wanted


def scatter_kernel(stride, flat_ref, rows_ref, *outs):
    for chunk, out in enumerate(outs):
        both = hits_of(flat_ref, chunk, stride, 0, stride) | hits_of(flat_ref, chunk, stride, 1, stride)
        out[...] = dot(both.astype(f32).astype(bf16), rows_ref[...], TN).astype(bf16)


def scatter_rows(flat, rows, experts, stride):
    features = rows.shape[1]
    return pl.pallas_call(
        functools.partial(scatter_kernel, stride),
        out_shape=[shaped((stride, features), bf16)] * experts,
        name="scatter_rows",
    )(flat, rows)


def gates_of(logits, experts):
    lane = lax.broadcasted_iota(jnp.int32, logits.shape, 1)
    logits = jnp.where(lane < experts, logits, -1e30)
    powers = jnp.exp(logits - jnp.max(logits, axis=1, keepdims=True))
    return powers / jnp.sum(powers, axis=1, keepdims=True)


def choice_of(ids_ref, k):
    lane = lax.broadcasted_iota(jnp.int32, (1, LANES), 1)
    return ids_ref[:, k : k + 1] == lane


def middle_kernel(experts, stride, capacity, offsets_ref, *refs):
    inputs = 6
    att_ref, x_ref, router_ref, par_ref, flat_ref, ids_ref = refs[:inputs]
    outs = refs[len(refs) - 4 - experts :]
    pieces = refs[inputs : len(refs) - 4 - experts]
    w_ref, residual_ref, two_ref, gate_ref = outs[:4]
    chunks = outs[4:]
    place(pieces, offsets_ref, w_ref)
    residual = x_ref[...].astype(f32) + dot(att_ref[...], w_ref[...], NN) + par_ref[6:7]
    residual_ref[...] = residual
    hat, _ = normalise(residual)
    two_ref[...] = (hat * par_ref[1:2] + par_ref[3:4]).astype(bf16)
    gates = gates_of(dot(two_ref[...], router_ref[...], NN), experts)
    gate_ref[...] = gates
    chosen = [
        jnp.sum(jnp.where(choice_of(ids_ref, k), gates, 0.0), axis=1, keepdims=True)
        for k in range(2)
    ]
    features = x_ref.shape[1]
    row = lax.broadcasted_iota(jnp.int32, (stride, 1), 0)
    blank = jnp.zeros((1, features - 3 * LANES), f32)
    for chunk, out in enumerate(chunks):
        wide = [hits_of(flat_ref, chunk, stride, k, LANES) for k in range(2)]
        slot_gate = jnp.sum(
            jnp.where(wide[0], chosen[0], 0.0) + jnp.where(wide[1], chosen[1], 0.0),
            axis=0,
            keepdims=True,
        )
        high = slot_gate.astype(bf16).astype(f32)
        rest = slot_gate - high
        middle = rest.astype(bf16).astype(f32)
        gate_row = jnp.concatenate([high, middle, rest - middle, blank], axis=1)
        both = hits_of(flat_ref, chunk, stride, 0, stride) | hits_of(flat_ref, chunk, stride, 1, stride)
        moved = dot(both.astype(f32).astype(bf16), two_ref[...], TN)
        out[...] = jnp.where(row == capacity, gate_row, moved).astype(bf16)


def middle(att, x, first_full, par, flat, ids, pieces, offsets, experts, stride, capacity):
    tokens, features = x.shape
    column = first_full.shape[1] // LANES - 1
    return pl.pallas_call(
        functools.partial(middle_kernel, experts, stride, capacity),
        grid_spec=pltpu.PrefetchScalarGridSpec(
            num_scalar_prefetch=1,
            grid=(1,),
            in_specs=[
                full(att.shape),
                full(x.shape),
                pl.BlockSpec((features, LANES), lambda i, o: (0, column)),
                full(par.shape),
                full(flat.shape),
                full(ids.shape),
            ]
            + [full(piece.shape) for piece in pieces],
            out_specs=[
                full((features, features)),
                full((tokens, features)),
                full((tokens, features)),
                full((tokens, LANES)),
            ]
            + [full((stride, features))] * experts,
        ),
        out_shape=[
            shaped((features, features), bf16),
            shaped((tokens, features), f32),
            shaped((tokens, features), bf16),
            shaped((tokens, LANES), f32),
        ]
        + [shaped((stride, features), bf16)] * experts,
        cost_estimate=pl.CostEstimate(
            flops=8 * tokens * features * features, bytes_accessed=8 << 20, transcendentals=0
        ),
        name="middle",
    )(offsets, att, x, first_full, par, flat, ids, *pieces)


GELU_A = 0.7978845608028654
GELU_B = 0.044715


def gelu_half(v):
    return 0.5 + 0.5 * jnp.tanh(v * (GELU_A + (GELU_A * GELU_B) * (v * v)))


def gelu_slope(v):
    square = v * v
    half = 0.5 + 0.5 * jnp.tanh(v * (GELU_A + (GELU_A * GELU_B) * square))
    bend = (v * half) * (1.0 - half)
    return half + bend * (2.0 * GELU_A + (6.0 * GELU_A * GELU_B) * square)


def expert_forward_kernel(count, capacity, *refs):
    xs, gs = refs[:count], refs[count : 2 * count]
    up_ref, bias_ref, x_ref, sg_ref, hid_ref, pre_ref, grad_ref = refs[2 * count :]
    stride = xs[0].shape[0]
    slots = x_ref.shape[0]

    @pl.when(pl.program_id(0) == 0)
    def _():
        eye = lax.broadcasted_iota(jnp.int32, (stride, LANES), 0) == lax.broadcasted_iota(
            jnp.int32, (stride, LANES), 1
        )
        for d in range(count):
            rows = slice(d * stride, (d + 1) * stride)
            x_ref[rows, :] = xs[d][...]
            tail = xs[d][stride - 16 :, :].astype(f32)
            at = capacity - (stride - 16)
            parts = tail[at : at + 1]
            gate = parts[:, :LANES] + parts[:, LANES : 2 * LANES] + parts[:, 2 * LANES : 3 * LANES]
            gate = jnp.sum(jnp.where(eye, gate, 0.0), axis=1, keepdims=True)
            sg_ref[rows, :] = (gate * gs[d][...].astype(f32)).astype(bf16)

    block = 256
    for m in range(0, slots, block):
        rows = slice(m, m + block)
        v = dot(x_ref[rows, :], up_ref[...], NN) + bias_ref[...]
        hid_ref[rows, :] = (v * gelu_half(v)).astype(bf16)
        pre_ref[rows, :] = v.astype(bf16)
    for n in range(0, hid_ref.shape[1], block):
        cols = slice(n, n + block)
        grad_ref[cols, :] = dot(hid_ref[:, cols], sg_ref[...], TN).astype(bf16)


def expert_forward(xs, gs, up, up_bias, capacity, tile=768):
    count = len(xs)
    stride, features = xs[0].shape
    slots, units = count * stride, up.shape[1]
    return pl.pallas_call(
        functools.partial(expert_forward_kernel, count, capacity),
        grid=(units // tile,),
        in_specs=[full((stride, features))] * (2 * count)
        + [
            pl.BlockSpec((features, tile), lambda j: (0, j)),
            pl.BlockSpec((1, tile), lambda j: (0, j)),
        ],
        out_specs=[
            full((slots, features)),
            full((slots, features)),
            pl.BlockSpec((slots, tile), lambda j: (0, j)),
            pl.BlockSpec((slots, tile), lambda j: (0, j)),
            pl.BlockSpec((tile, features), lambda j: (j, 0)),
        ],
        out_shape=[
            shaped((slots, features), bf16),
            shaped((slots, features), bf16),
            shaped((slots, units), bf16),
            shaped((slots, units), bf16),
            shaped((units, features), bf16),
        ],
        cost_estimate=pl.CostEstimate(
            flops=4 * slots * features * units, bytes_accessed=30 << 20, transcendentals=0
        ),
        name="expert_forward",
    )(*xs, *gs, up, up_bias)


def accumulate(acc_ref, value, initial=None):
    @pl.when(pl.program_id(0) == 0)
    def _():
        acc_ref[...] = value if initial is None else value + initial

    @pl.when(pl.program_id(0) > 0)
    def _():
        acc_ref[...] += value


def emit_chunks(acc_ref, outs):
    @pl.when(pl.program_id(0) == pl.num_programs(0) - 1)
    def _():
        stride = acc_ref.shape[0] // len(outs)
        for d, out in enumerate(outs):
            out[...] = acc_ref[d * stride : (d + 1) * stride, :].astype(bf16)


def expert_out_kernel(count, hid_ref, down_ref, bias_ref, *refs):
    outs, acc_ref = refs[:count], refs[count]
    accumulate(acc_ref, dot(hid_ref[...], down_ref[...], NN), bias_ref[...])
    emit_chunks(acc_ref, outs)


def expert_out(hidden, down, bias, count, tile=768):
    slots, units = hidden.shape
    features = down.shape[1]
    return pl.pallas_call(
        functools.partial(expert_out_kernel, count),
        grid=(units // tile,),
        in_specs=[
            pl.BlockSpec((slots, tile), lambda j: (0, j)),
            pl.BlockSpec((tile, features), lambda j: (j, 0)),
            full((1, features)),
        ],
        out_specs=[full((slots // count, features))] * count,
        out_shape=[shaped((slots // count, features), bf16)] * count,
        scratch_shapes=[pltpu.VMEM((slots, features), f32)],
        cost_estimate=pl.CostEstimate(
            flops=2 * slots * features * units, bytes_accessed=12 << 20, transcendentals=0
        ),
        name="expert_out",
    )(hidden, down, bias)


def expert_back_kernel(count, sg_ref, down_ref, pre_ref, up_ref, inner_ref, sums_ref, *refs):
    outs, acc_ref = refs[:count], refs[count]
    slots, block = acc_ref.shape[0], 256
    total = jnp.zeros(sums_ref.shape, f32)
    for m in range(0, slots, block):
        rows = slice(m, m + block)
        slope = gelu_slope(pre_ref[rows, :].astype(f32))
        low = (dot(sg_ref[rows, :], down_ref[...], NT) * slope).astype(bf16)
        inner_ref[rows, :] = low
        total += jnp.sum(low.astype(f32), axis=0, keepdims=True)
    sums_ref[...] = total
    accumulate(acc_ref, dot(inner_ref[...], up_ref[...], NT))
    emit_chunks(acc_ref, outs)


def expert_back(slot_grad, down, pre, up, count, tile=768):
    slots, features = slot_grad.shape
    units = up.shape[1]
    return pl.pallas_call(
        functools.partial(expert_back_kernel, count),
        grid=(units // tile,),
        in_specs=[
            full((slots, features)),
            pl.BlockSpec((tile, features), lambda j: (j, 0)),
            pl.BlockSpec((slots, tile), lambda j: (0, j)),
            pl.BlockSpec((features, tile), lambda j: (0, j)),
        ],
        out_specs=[
            pl.BlockSpec((slots, tile), lambda j: (0, j)),
            pl.BlockSpec((1, tile), lambda j: (0, j)),
        ]
        + [full((slots // count, features))] * count,
        out_shape=[shaped((slots, units), bf16), shaped((1, units), f32)]
        + [shaped((slots // count, features), bf16)] * count,
        scratch_shapes=[pltpu.VMEM((slots, features), f32)],
        cost_estimate=pl.CostEstimate(
            flops=4 * slots * features * units, bytes_accessed=24 << 20, transcendentals=0
        ),
        name="expert_back",
    )(slot_grad, down, pre, up)


def up_gradient_kernel(x_ref, inner_ref, out_ref):
    block = 256
    for n in range(0, x_ref.shape[1], block):
        cols = slice(n, n + block)
        out_ref[cols, :] = dot(x_ref[:, cols], inner_ref[...], TN).astype(bf16)


def up_gradient(x, inner, tile=768):
    slots, features = x.shape
    units = inner.shape[1]
    return pl.pallas_call(
        up_gradient_kernel,
        grid=(units // tile,),
        in_specs=[full((slots, features)), pl.BlockSpec((slots, tile), lambda j: (0, j))],
        out_specs=pl.BlockSpec((features, tile), lambda j: (0, j)),
        out_shape=shaped((features, units), bf16),
        cost_estimate=pl.CostEstimate(
            flops=2 * slots * features * units, bytes_accessed=12 << 20, transcendentals=0
        ),
        name="up_gradient",
    )(x, inner)


def combine_kernel(experts, stride, *refs):
    chunks = refs[:experts]
    flat_ref, ids_ref, gate_ref, residual_ref, grad_ref, out_ref, logit_ref = refs[experts:-1]
    rows_ref = refs[-1]
    for d in range(experts):
        rows_ref[d * stride : (d + 1) * stride, :] = chunks[d][...]
    slots = experts * stride
    slot = lax.broadcasted_iota(jnp.int32, (1, slots), 1)
    gates = gate_ref[...]
    grads = grad_ref[...].astype(f32)
    total = residual_ref[...]
    mass = jnp.zeros_like(gates)
    for k in range(2):
        hits = (flat_ref[:, k : k + 1] == slot).astype(f32).astype(bf16)
        picked = dot(hits, rows_ref[...], NN)
        choice = choice_of(ids_ref, k)
        total += jnp.sum(jnp.where(choice, gates, 0.0), axis=1, keepdims=True) * picked
        gate_grad = jnp.sum(grads * picked, axis=1, keepdims=True)
        mass += jnp.where(choice, gate_grad, 0.0)
    out_ref[...] = total.astype(bf16)
    logit_ref[...] = (gates * (mass - jnp.sum(gates * mass, axis=1, keepdims=True))).astype(bf16)


def combine(chunks, flat, ids, gates, residual, grad_low):
    experts, (stride, features) = len(chunks), chunks[0].shape
    tokens = residual.shape[0]
    return pl.pallas_call(
        functools.partial(combine_kernel, experts, stride),
        out_shape=[shaped((tokens, features), bf16), shaped((tokens, LANES), bf16)],
        scratch_shapes=[pltpu.VMEM((experts * stride, features), bf16)],
        cost_estimate=pl.CostEstimate(
            flops=4 * tokens * experts * stride * features, bytes_accessed=6 << 20, transcendentals=0
        ),
        name="combine",
    )(*chunks, flat, ids, gates, residual, grad_low)


def split_rows(value_ref, offsets_ref, width, kept_ref, sent_ref):
    blocks = 2 * kept_ref.shape[0]
    rows = kept_ref.shape[1]
    for d in range(blocks):
        part = value_ref[pl.ds(pl.multiple_of(offsets_ref[d], 8), rows), :].astype(bf16)
        (kept_ref, sent_ref)[d % 2][d // 2, :, width] = part


def residual_back_kernel(experts, stride, offsets_ref, *refs):
    chunks = refs[:experts]
    (
        flat_ref,
        logit_ref,
        router_ref,
        two_ref,
        residual_ref,
        grad_ref,
        par_ref,
        w_ref,
        att_ref,
        residual_grad_ref,
        att_grad_ref,
        kept_ref,
        sent_ref,
        rows_ref,
        vector_ref,
        value_ref,
        small_ref,
    ) = refs[experts:]
    for d in range(experts):
        rows_ref[d * stride : (d + 1) * stride, :] = chunks[d][...]
    features = residual_ref.shape[1]
    slot = lax.broadcasted_iota(jnp.int32, (1, experts * stride), 1)
    hits = (flat_ref[:, 0:1] == slot) | (flat_ref[:, 1:2] == slot)
    two_grad = dot(hits.astype(f32).astype(bf16), rows_ref[...], NN)
    two_grad += dot(logit_ref[...], router_ref[...], NT)
    hat, scale = normalise(residual_ref[...])
    residual_grad = grad_ref[...].astype(f32) + normalise_back(two_grad, hat, scale, par_ref[1:2])
    residual_grad_ref[...] = residual_grad
    branch = residual_grad.astype(bf16)
    vector_ref[...] = jnp.zeros_like(vector_ref)
    vector_ref[0:1] = jnp.sum(two_grad * hat, axis=0, keepdims=True)
    vector_ref[1:2] = jnp.sum(two_grad, axis=0, keepdims=True)
    vector_ref[2:3] = jnp.sum(residual_grad, axis=0, keepdims=True)
    att_grad_ref[...] = dot(branch, w_ref[...], NT).astype(bf16)
    value_ref[...] = dot(att_ref[...], branch, TN)
    split_rows(value_ref, offsets_ref, slice(0, features), kept_ref, sent_ref)
    small_ref[...] = dot(two_ref[...], logit_ref[...], TN)
    split_rows(small_ref, offsets_ref, slice(features, features + LANES), kept_ref, sent_ref)
    small_ref[...] = jnp.transpose(vector_ref[...])
    split_rows(
        small_ref, offsets_ref, slice(features + LANES, features + 2 * LANES), kept_ref, sent_ref
    )


def residual_back(
    chunks, flat, logit_grad, first_full, two, residual, grad_low, par, w, att, offsets
):
    experts, (stride, features) = len(chunks), chunks[0].shape
    tokens = residual.shape[0]
    column = first_full.shape[1] // LANES - 1
    size = offsets.shape[0]
    packed = (size // 2, features // size, features + 2 * LANES)
    return pl.pallas_call(
        functools.partial(residual_back_kernel, experts, stride),
        grid_spec=pltpu.PrefetchScalarGridSpec(
            num_scalar_prefetch=1,
            grid=(1,),
            in_specs=[full((stride, features))] * experts
            + [
                full(flat.shape),
                full(logit_grad.shape),
                pl.BlockSpec((features, LANES), lambda i, o: (0, column)),
            ]
            + [full(value.shape) for value in (two, residual, grad_low, par, w, att)],
            out_specs=[full((tokens, features))] * 2 + [full(packed)] * 2,
            scratch_shapes=[
                pltpu.VMEM((experts * stride, features), bf16),
                pltpu.VMEM((LANES, features), f32),
                pltpu.VMEM((features, features), f32),
                pltpu.VMEM((features, LANES), f32),
            ],
        ),
        out_shape=[
            shaped((tokens, features), f32),
            shaped((tokens, features), bf16),
            shaped(packed, bf16),
            shaped(packed, bf16),
        ],
        cost_estimate=pl.CostEstimate(
            flops=8 * tokens * features * features, bytes_accessed=10 << 20, transcendentals=0
        ),
        name="residual_back",
    )(
        offsets, *chunks, flat, logit_grad, first_full, two, residual, grad_low, par, w, att
    )


def attend_back_kernel(proj_ref, prob_ref, out_grad_ref, grad_ref):
    features = out_grad_ref.shape[1]
    low = lax.broadcasted_iota(jnp.int32, (1, LANES), 1) < HEAD_DIM

    def pair(p, carry):
        def cols(third):
            return pl.ds(pl.multiple_of(third * features + p * LANES, LANES), LANES)

        query, key, value = (proj_ref[:, cols(third)] for third in range(3))
        grads = out_grad_ref[:, cols(0)]
        results = []
        for half in range(2):
            mine = low if half == 0 else ~low
            low_probs = prob_ref[2 * p + half]
            probs = low_probs.astype(f32)
            weight_grad = dot(jnp.where(mine, grads, jnp.zeros_like(grads)), value, NT)
            total = jnp.sum(weight_grad * probs, axis=1, keepdims=True)
            score_grad = (probs * (weight_grad - total)).astype(bf16)
            results.append(
                (
                    dot(score_grad, key, NN) * HEAD_DIM**-0.5,
                    dot(score_grad, query, TN) * HEAD_DIM**-0.5,
                    dot(low_probs, grads, TN),
                )
            )
        for third in range(3):
            grad_ref[:, cols(third)] = jnp.where(
                low, results[0][third], results[1][third]
            ).astype(bf16)
        return carry

    lax.fori_loop(0, features // LANES, pair, 0, unroll=3)


def attend_back(proj, probs, out_grad, images):
    tokens, features = out_grad.shape
    padded = tokens // images
    image = lambda i: (i, 0)
    return pl.pallas_call(
        attend_back_kernel,
        grid=(images,),
        in_specs=[
            pl.BlockSpec((padded, 3 * features), image),
            pl.BlockSpec((HEADS, padded, padded), lambda i: (i, 0, 0)),
            pl.BlockSpec((padded, features), image),
        ],
        out_specs=pl.BlockSpec((padded, 3 * features), image),
        out_shape=shaped((tokens, 3 * features), bf16),
        cost_estimate=pl.CostEstimate(
            flops=12 * tokens * features * features, bytes_accessed=6 << 20, transcendentals=0
        ),
        name="attend_back",
    )(proj, probs, out_grad)


def input_back_kernel(
    offsets_ref,
    norm_ref,
    grad_ref,
    w_ref,
    x_ref,
    residual_grad_ref,
    par_ref,
    out_ref,
    kept_ref,
    sent_ref,
    acc_ref,
    vector_ref,
    value_ref,
    small_ref,
):
    features = x_ref.shape[1]
    vector_ref[...] = jnp.zeros_like(vector_ref)
    for third in range(3):
        cols = slice(third * features, (third + 1) * features)
        value_ref[...] = dot(norm_ref[...], grad_ref[:, cols], TN)
        split_rows(value_ref, offsets_ref, cols, kept_ref, sent_ref)
        value = dot(grad_ref[:, cols], w_ref[:, cols], NT)
        if third == 0:
            acc_ref[...] = value
        else:
            acc_ref[...] += value
        if third != 1:
            row = 2 + third // 2
            vector_ref[row : row + 1] = jnp.sum(
                grad_ref[:, cols].astype(f32), axis=0, keepdims=True
            )
    hat, scale = normalise(x_ref[...].astype(f32))
    grads = acc_ref[...]
    vector_ref[0:1] = jnp.sum(grads * hat, axis=0, keepdims=True)
    vector_ref[1:2] = jnp.sum(grads, axis=0, keepdims=True)
    small_ref[...] = jnp.transpose(vector_ref[...])
    split_rows(
        small_ref, offsets_ref, slice(3 * features, 3 * features + LANES), kept_ref, sent_ref
    )
    out_ref[...] = (
        residual_grad_ref[...] + normalise_back(grads, hat, scale, par_ref[0:1])
    ).astype(bf16)


def input_back(norm, grads, first_full, x, residual_grad, par, offsets):
    tokens, features = x.shape
    size = offsets.shape[0]
    packed = (size // 2, features // size, 3 * features + LANES)
    return pl.pallas_call(
        input_back_kernel,
        grid_spec=pltpu.PrefetchScalarGridSpec(
            num_scalar_prefetch=1,
            grid=(1,),
            in_specs=[full(norm.shape), full(grads.shape), full((features, 3 * features))]
            + [full(value.shape) for value in (x, residual_grad, par)],
            out_specs=[full((tokens, features))] + [full(packed)] * 2,
            scratch_shapes=[
                pltpu.VMEM((tokens, features), f32),
                pltpu.VMEM((LANES, features), f32),
                pltpu.VMEM((features, features), f32),
                pltpu.VMEM((features, LANES), f32),
            ],
        ),
        out_shape=[shaped((tokens, features), bf16), shaped(packed, bf16), shaped(packed, bf16)],
        cost_estimate=pl.CostEstimate(
            flops=12 * tokens * features * features, bytes_accessed=16 << 20, transcendentals=0
        ),
        name="input_back",
    )(offsets, norm, grads, first_full, x, residual_grad, par)


def reduce_blocks(kept, sent, expert_size, dp_size, dp_index):
    pair_sum = (
        kept.astype(f32) + swap(sent, "expert", expert_size, 1).astype(f32)
    ).astype(bf16)
    parts = [pair_sum[0]] + [
        swap(pair_sum[d // 2], "expert", expert_size, d) for d in range(2, expert_size, 2)
    ]
    plane_sum = sum(part.astype(f32) for part in parts).astype(bf16)
    plane_sum = plane_sum.reshape(dp_size, plane_sum.shape[0] // dp_size, -1)
    dp_parts = exchange(
        [
            lax.dynamic_index_in_dim(plane_sum, dp_index ^ d, 0, keepdims=False)
            for d in range(dp_size)
        ],
        "dp",
        dp_size,
    )
    dp_sum = sum(part.astype(f32) for part in dp_parts).astype(bf16)
    return lax.all_gather(dp_sum, "dp", axis=0, tiled=True).astype(f32)


def per_device(
    block_input,
    out_grad,
    expert_ids,
    slot_order,
    joint_weight,
    out_weight,
    router_weight,
    norm_gains,
    norm_shifts,
    attention_bias,
    up_weight,
    down_weight,
    up_bias,
    down_bias,
    *,
    expert_size,
    dp_size,
):
    index = lax.axis_index("expert")
    dp_index = lax.axis_index("dp")
    row_count, features = block_input.shape
    images = row_count // SEQ
    experts = router_weight.shape[1]
    capacity = max(2, (5 * row_count + 2 * experts - 1) // (2 * experts))
    stride = round_up(capacity + 1, 16)
    slots = experts * stride
    padded = round_up(SEQ, 16)
    tokens = images * padded
    hidden_units = up_weight.shape[2]
    block_rows = features // expert_size
    row_offsets = (index ^ jnp.arange(expert_size, dtype=jnp.int32)) * block_rows

    def pad_rows(values, fill=0):
        split = values.reshape(images, SEQ, values.shape[-1])
        return jnp.pad(
            split, ((0, 0), (0, padded - SEQ), (0, 0)), constant_values=fill
        ).reshape(tokens, values.shape[-1])

    def crop_rows(values):
        return values.reshape(images, padded, -1)[:, :SEQ].reshape(row_count, -1)

    small = jnp.concatenate(
        [router_weight, norm_gains.T, norm_shifts.T, attention_bias.T], axis=1
    )
    small = jnp.pad(small, ((0, 0), (0, LANES - small.shape[1])))
    first, first_offsets = gather_pieces(
        jnp.concatenate([joint_weight, small], axis=1), "expert", expert_size
    )
    input_low, grad_low = pad_rows(block_input), pad_rows(out_grad)
    ids = pad_rows(expert_ids)
    flat = pad_rows(
        slot_index(expert_ids, slot_order[0], experts, capacity, stride, index), slots
    )
    grad_slots = scatter_rows(flat, grad_low, experts, stride)
    first, grad_slots, out_shard = lax.optimization_barrier((first, grad_slots, out_weight))
    second, second_offsets = gather_pieces(out_shard, "expert", expert_size)
    grad_arrived = exchange(grad_slots, "expert", expert_size)

    first_full, par, normed, projected, probs, attended = attend(
        input_low, first, first_offsets, experts, images
    )
    out_full, residual, two_low, gates, *dispatched = middle(
        attended,
        input_low,
        first_full,
        par,
        flat,
        ids,
        second,
        second_offsets,
        experts,
        stride,
        capacity,
    )
    arrived = exchange(dispatched, "expert", expert_size)

    up, down = up_weight[0], down_weight[0]
    rows, slot_grad, hidden, pre, down_local = expert_forward(
        arrived, grad_arrived, up, up_bias.astype(f32), capacity
    )
    down_part = lax.psum_scatter(down_local, "dp", scatter_dimension=0, tiled=True)
    expert_low = expert_out(hidden, down, down_bias.astype(f32), experts)
    slot_grad, expert_low = lax.optimization_barrier((slot_grad, expert_low))
    returned = exchange(expert_low, "expert", expert_size)
    inner, inner_sums, *rows_grad = expert_back(slot_grad, down, pre, up, experts)
    rows_back = exchange(rows_grad, "expert", expert_size)
    up_local = up_gradient(rows, inner)
    up_part = lax.psum_scatter(up_local, "dp", scatter_dimension=1, tiled=True)
    bias_local = jnp.concatenate(
        [
            inner_sums.reshape(dp_size, -1),
            jnp.sum(slot_grad, axis=0, dtype=f32).reshape(dp_size, -1),
        ],
        axis=1,
    )
    bias_chunks = [
        lax.dynamic_index_in_dim(bias_local, dp_index ^ d, 0) for d in range(dp_size)
    ]
    bias_sum = sum(exchange(bias_chunks, "dp", dp_size))
    up_bias_grad = bias_sum[:, : hidden_units // dp_size]
    down_bias_grad = bias_sum[:, hidden_units // dp_size :]

    block_output, logit_grad = combine(returned, flat, ids, gates, residual, grad_low)
    residual_grad, attended_grad, kept, sent = residual_back(
        rows_back,
        flat,
        logit_grad,
        first_full,
        two_low,
        residual,
        grad_low,
        par,
        out_full,
        attended,
        row_offsets,
    )
    late = reduce_blocks(kept, sent, expert_size, dp_size, dp_index)
    projected_grad = attend_back(projected, probs, attended_grad, images)
    input_grad, kept, sent = input_back(
        normed, projected_grad, first_full, input_low, residual_grad, par, row_offsets
    )
    early = reduce_blocks(kept, sent, expert_size, dp_size, dp_index)
    late_vectors = late[:, features + LANES : features + LANES + 3].T
    early_vectors = early[:, 3 * features : 3 * features + 4].T
    return (
        crop_rows(block_output),
        crop_rows(input_grad),
        early[:, : 3 * features],
        late[:, :features],
        late[:, features : features + experts],
        jnp.stack([early_vectors[0], late_vectors[0]]),
        jnp.stack([early_vectors[1], late_vectors[1]]),
        jnp.stack([early_vectors[2], early_vectors[3], late_vectors[2]]),
        up_part[None].astype(f32),
        down_part[None].astype(f32),
        up_bias_grad,
        down_bias_grad,
    )


def solution(mesh):
    def body(*args):
        return per_device(
            *args, expert_size=mesh.shape["expert"], dp_size=mesh.shape["dp"]
        )

    in_specs = (
        P(("dp", "expert"), None),
        P(("dp", "expert"), None),
        P(("dp", "expert"), None),
        P(("dp", "expert"), None),
        P("expert", None),
        P("expert", None),
        P("expert", None),
        P(None, "expert"),
        P(None, "expert"),
        P(None, "expert"),
        P("expert", None, None),
        P("expert", None, None),
        P("expert", None),
        P("expert", None),
    )
    out_specs = (
        P(("dp", "expert"), None),
        P(("dp", "expert"), None),
        P("expert", None),
        P("expert", None),
        P("expert", None),
        P(None, "expert"),
        P(None, "expert"),
        P(None, "expert"),
        P("expert", None, "dp"),
        P("expert", "dp", None),
        P("expert", "dp"),
        P("expert", "dp"),
    )
    return jax.shard_map(
        body, mesh=mesh, in_specs=in_specs, out_specs=out_specs, check_vma=False
    )
```

```python
import functools

import jax
import jax.numpy as jnp
from jax import lax
from jax.experimental import pallas as pl
from jax.experimental.pallas import tpu as pltpu
from jax.sharding import PartitionSpec as P


HEADS = 12
HEAD_DIM = 64
SEQ = 197
LANES = 128
norm_eps = 1e-06


f32 = jnp.float32
bf16 = jnp.bfloat16
NN = ((1,), (0,))
NT = ((1,), (1,))
TN = ((0,), (0,))


def round_up(value, step):
    return (value + step - 1) // step * step


def dot(left, right, dims):
    return lax.dot_general(left, right, (dims, ((), ())), preferred_element_type=f32)


def swap(value, axis, size, offset):
    return lax.ppermute(value, axis, [(i, i ^ offset) for i in range(size)])


def exchange(chunks, axis, size):
    return [chunks[0]] + [swap(chunks[d], axis, size, d) for d in range(1, size)]


def gather_pieces(shard, axis, size):
    rows = shard.shape[0]
    if rows % 16:
        return [lax.all_gather(shard, axis, axis=0, tiled=True)], jnp.zeros((1,), jnp.int32)
    same = [shard] + [swap(shard, axis, size, d) for d in range(2, size, 2)]
    other = [swap(part, axis, size, 1) for part in same]
    pieces = [(same, other)[d % 2][d // 2] for d in range(size)]
    offsets = (lax.axis_index(axis) ^ jnp.arange(size, dtype=jnp.int32)) * rows
    return pieces, offsets


def normalise(values):
    row_mean = jnp.mean(values, axis=-1, keepdims=True)
    centered = values - row_mean
    row_var = jnp.mean(centered * centered, axis=-1, keepdims=True)
    scale = lax.rsqrt(row_var + norm_eps)
    return centered * scale, scale


def normalise_back(grads, hat, scale, gain):
    u = grads * gain
    return scale * (
        u
        - jnp.mean(u, axis=-1, keepdims=True)
        - hat * jnp.mean(u * hat, axis=-1, keepdims=True)
    )


def slot_index(ids, order, experts, capacity, stride, index):
    tokens = ids.shape[0]
    place = jnp.arange(tokens, dtype=jnp.int32)
    hits = order[:, None] == place[None, :]
    position = jnp.sum(jnp.where(hits, place[:, None], 0), axis=0)
    position_row = jnp.sum(jnp.where(hits.T, place[None, :], 0), axis=1)
    earlier = (position_row[None, :] < position[:, None]).astype(bf16)
    expert_iota = jnp.arange(experts, dtype=jnp.int32)
    hot = [(ids[:, k : k + 1] == expert_iota[None, :]) for k in range(2)]
    counts = dot(
        earlier, jnp.concatenate(hot, axis=1).astype(bf16), ((1,), (0,))
    )
    base = jnp.sum(hot[0].astype(f32), axis=0, keepdims=True)
    first = jnp.sum(jnp.where(hot[0], counts[:, :experts], 0.0), axis=1)
    second = jnp.sum(jnp.where(hot[1], counts[:, experts:] + base, 0.0), axis=1)
    rank = jnp.stack([first, second], axis=1).astype(jnp.int32)
    return jnp.where(rank < capacity, (ids ^ index) * stride + rank, experts * stride)


def shaped(shape, dtype):
    return jax.ShapeDtypeStruct(shape, dtype)


def full(shape):
    return pl.BlockSpec(shape, lambda *_: (0,) * len(shape))


def place(pieces, offsets_ref, out_ref):
    rows = pieces[0].shape[0]
    for k, piece in enumerate(pieces):
        out_ref[pl.ds(pl.multiple_of(offsets_ref[k], 16), rows), :] = piece[...]


def attend_kernel(experts, padded, offsets_ref, x_ref, *refs):
    pieces = refs[:-6]
    w_ref, par_ref, norm_ref, proj_ref, prob_ref, att_ref = refs[-6:]
    features = x_ref.shape[1]

    @pl.when(pl.program_id(0) == 0)
    def _():
        place(pieces, offsets_ref, w_ref)
        par = jnp.transpose(w_ref[:, 3 * features :].astype(f32))
        par_ref[...] = par[experts : experts + 8]

    hat, _ = normalise(x_ref[...].astype(f32))
    norm_ref[...] = (hat * par_ref[0:1] + par_ref[2:3]).astype(bf16)
    zero = jnp.zeros((1, features), f32)
    for third, bias in enumerate((par_ref[4:5], zero, par_ref[5:6])):
        cols = slice(third * features, (third + 1) * features)
        proj_ref[:, cols] = (dot(norm_ref[...], w_ref[:, cols], NN) + bias).astype(bf16)
    low = lax.broadcasted_iota(jnp.int32, (1, LANES), 1) < HEAD_DIM
    valid = lax.broadcasted_iota(jnp.int32, (1, padded), 1) < SEQ

    def pair(p, carry):
        def cols(third):
            return pl.ds(pl.multiple_of(third * features + p * LANES, LANES), LANES)

        query, key, value = (proj_ref[:, cols(third)] for third in range(3))
        query = query * jnp.asarray(HEAD_DIM**-0.5, bf16)
        outs = []
        for half in range(2):
            mine = low if half == 0 else ~low
            scores = dot(jnp.where(mine, query, jnp.zeros_like(query)), key, NT)
            scores = jnp.where(valid, scores, -1e30)
            powers = jnp.exp(scores - jnp.max(scores, axis=1, keepdims=True))
            probs = (powers * (1.0 / jnp.sum(powers, axis=1, keepdims=True))).astype(bf16)
            prob_ref[2 * p + half] = probs
            outs.append(dot(probs, value, NN))
        att_ref[:, cols(0)] = jnp.where(low, outs[0], outs[1]).astype(bf16)
        return carry

    lax.fori_loop(0, features // LANES, pair, 0, unroll=3)


def attend(x, pieces, offsets, experts, images):
    tokens, features = x.shape
    padded = tokens // images
    width = pieces[0].shape[1]
    image = lambda i, o: (i, 0)
    return pl.pallas_call(
        functools.partial(attend_kernel, experts, padded),
        grid_spec=pltpu.PrefetchScalarGridSpec(
            num_scalar_prefetch=1,
            grid=(images,),
            in_specs=[pl.BlockSpec((padded, features), image)]
            + [full(piece.shape) for piece in pieces],
            out_specs=[
                full((features, width)),
                full((8, features)),
                pl.BlockSpec((padded, features), image),
                pl.BlockSpec((padded, 3 * features), image),
                pl.BlockSpec((HEADS, padded, padded), lambda i, o: (i, 0, 0)),
                pl.BlockSpec((padded, features), image),
            ],
        ),
        out_shape=[
            shaped((features, width), bf16),
            shaped((8, features), f32),
            shaped((tokens, features), bf16),
            shaped((tokens, 3 * features), bf16),
            shaped((images * HEADS, padded, padded), bf16),
            shaped((tokens, features), bf16),
        ],
        cost_estimate=pl.CostEstimate(
            flops=12 * tokens * features * features, bytes_accessed=16 << 20, transcendentals=0
        ),
        name="attend",
    )(offsets, x, *pieces)


def hits_of(flat_ref, chunk, stride, k, width):
    lane = lax.broadcasted_iota(jnp.int32, (1, width), 1)
    wanted = jnp.where(lane < stride, lane + chunk * stride, -1)
    return flat_ref[:, k : k + 1] == wanted


def scatter_kernel(stride, flat_ref, rows_ref, *outs):
    for chunk, out in enumerate(outs):
        both = hits_of(flat_ref, chunk, stride, 0, stride) | hits_of(flat_ref, chunk, stride, 1, stride)
        out[...] = dot(both.astype(f32).astype(bf16), rows_ref[...], TN).astype(bf16)


def scatter_rows(flat, rows, experts, stride):
    features = rows.shape[1]
    return pl.pallas_call(
        functools.partial(scatter_kernel, stride),
        out_shape=[shaped((stride, features), bf16)] * experts,
        name="scatter_rows",
    )(flat, rows)


def gates_of(logits, experts):
    lane = lax.broadcasted_iota(jnp.int32, logits.shape, 1)
    logits = jnp.where(lane < experts, logits, -1e30)
    powers = jnp.exp(logits - jnp.max(logits, axis=1, keepdims=True))
    return powers / jnp.sum(powers, axis=1, keepdims=True)


def choice_of(ids_ref, k):
    lane = lax.broadcasted_iota(jnp.int32, (1, LANES), 1)
    return ids_ref[:, k : k + 1] == lane


def middle_kernel(experts, stride, capacity, offsets_ref, *refs):
    inputs = 6
    att_ref, x_ref, router_ref, par_ref, flat_ref, ids_ref = refs[:inputs]
    outs = refs[len(refs) - 4 - experts :]
    pieces = refs[inputs : len(refs) - 4 - experts]
    w_ref, residual_ref, two_ref, gate_ref = outs[:4]
    chunks = outs[4:]
    place(pieces, offsets_ref, w_ref)
    residual = x_ref[...].astype(f32) + dot(att_ref[...], w_ref[...], NN) + par_ref[6:7]
    residual_ref[...] = residual
    hat, _ = normalise(residual)
    two_ref[...] = (hat * par_ref[1:2] + par_ref[3:4]).astype(bf16)
    gates = gates_of(dot(two_ref[...], router_ref[...], NN), experts)
    gate_ref[...] = gates
    chosen = [
        jnp.sum(jnp.where(choice_of(ids_ref, k), gates, 0.0), axis=1, keepdims=True)
        for k in range(2)
    ]
    features = x_ref.shape[1]
    row = lax.broadcasted_iota(jnp.int32, (stride, 1), 0)
    blank = jnp.zeros((1, features - 3 * LANES), f32)
    for chunk, out in enumerate(chunks):
        wide = [hits_of(flat_ref, chunk, stride, k, LANES) for k in range(2)]
        slot_gate = jnp.sum(
            jnp.where(wide[0], chosen[0], 0.0) + jnp.where(wide[1], chosen[1], 0.0),
            axis=0,
            keepdims=True,
        )
        high = slot_gate.astype(bf16).astype(f32)
        rest = slot_gate - high
        middle = rest.astype(bf16).astype(f32)
        gate_row = jnp.concatenate([high, middle, rest - middle, blank], axis=1)
        both = hits_of(flat_ref, chunk, stride, 0, stride) | hits_of(flat_ref, chunk, stride, 1, stride)
        moved = dot(both.astype(f32).astype(bf16), two_ref[...], TN)
        out[...] = jnp.where(row == capacity, gate_row, moved).astype(bf16)


def middle(att, x, first_full, par, flat, ids, pieces, offsets, experts, stride, capacity):
    tokens, features = x.shape
    column = first_full.shape[1] // LANES - 1
    return pl.pallas_call(
        functools.partial(middle_kernel, experts, stride, capacity),
        grid_spec=pltpu.PrefetchScalarGridSpec(
            num_scalar_prefetch=1,
            grid=(1,),
            in_specs=[
                full(att.shape),
                full(x.shape),
                pl.BlockSpec((features, LANES), lambda i, o: (0, column)),
                full(par.shape),
                full(flat.shape),
                full(ids.shape),
            ]
            + [full(piece.shape) for piece in pieces],
            out_specs=[
                full((features, features)),
                full((tokens, features)),
                full((tokens, features)),
                full((tokens, LANES)),
            ]
            + [full((stride, features))] * experts,
        ),
        out_shape=[
            shaped((features, features), bf16),
            shaped((tokens, features), f32),
            shaped((tokens, features), bf16),
            shaped((tokens, LANES), f32),
        ]
        + [shaped((stride, features), bf16)] * experts,
        cost_estimate=pl.CostEstimate(
            flops=8 * tokens * features * features, bytes_accessed=8 << 20, transcendentals=0
        ),
        name="middle",
    )(offsets, att, x, first_full, par, flat, ids, *pieces)


GELU_A = 0.7978845608028654
GELU_B = 0.044715


def gelu_half(v):
    return 0.5 + 0.5 * jnp.tanh(v * (GELU_A + (GELU_A * GELU_B) * (v * v)))


def gelu_slope(v):
    square = v * v
    half = 0.5 + 0.5 * jnp.tanh(v * (GELU_A + (GELU_A * GELU_B) * square))
    bend = (v * half) * (1.0 - half)
    return half + bend * (2.0 * GELU_A + (6.0 * GELU_A * GELU_B) * square)


def expert_forward_kernel(count, capacity, *refs):
    xs, gs = refs[:count], refs[count : 2 * count]
    up_ref, bias_ref, x_ref, sg_ref, hid_ref, pre_ref, grad_ref = refs[2 * count :]
    stride = xs[0].shape[0]
    slots = x_ref.shape[0]

    @pl.when(pl.program_id(0) == 0)
    def _():
        eye = lax.broadcasted_iota(jnp.int32, (stride, LANES), 0) == lax.broadcasted_iota(
            jnp.int32, (stride, LANES), 1
        )
        for d in range(count):
            rows = slice(d * stride, (d + 1) * stride)
            x_ref[rows, :] = xs[d][...]
            tail = xs[d][stride - 16 :, :].astype(f32)
            at = capacity - (stride - 16)
            parts = tail[at : at + 1]
            gate = parts[:, :LANES] + parts[:, LANES : 2 * LANES] + parts[:, 2 * LANES : 3 * LANES]
            gate = jnp.sum(jnp.where(eye, gate, 0.0), axis=1, keepdims=True)
            sg_ref[rows, :] = (gate * gs[d][...].astype(f32)).astype(bf16)

    block = 256
    for m in range(0, slots, block):
        rows = slice(m, m + block)
        v = dot(x_ref[rows, :], up_ref[...], NN) + bias_ref[...]
        hid_ref[rows, :] = (v * gelu_half(v)).astype(bf16)
        pre_ref[rows, :] = v.astype(bf16)
    for n in range(0, hid_ref.shape[1], block):
        cols = slice(n, n + block)
        grad_ref[cols, :] = dot(hid_ref[:, cols], sg_ref[...], TN).astype(bf16)


def expert_forward(xs, gs, up, up_bias, capacity, tile=768):
    count = len(xs)
    stride, features = xs[0].shape
    slots, units = count * stride, up.shape[1]
    return pl.pallas_call(
        functools.partial(expert_forward_kernel, count, capacity),
        grid=(units // tile,),
        in_specs=[full((stride, features))] * (2 * count)
        + [
            pl.BlockSpec((features, tile), lambda j: (0, j)),
            pl.BlockSpec((1, tile), lambda j: (0, j)),
        ],
        out_specs=[
            full((slots, features)),
            full((slots, features)),
            pl.BlockSpec((slots, tile), lambda j: (0, j)),
            pl.BlockSpec((slots, tile), lambda j: (0, j)),
            pl.BlockSpec((tile, features), lambda j: (j, 0)),
        ],
        out_shape=[
            shaped((slots, features), bf16),
            shaped((slots, features), bf16),
            shaped((slots, units), bf16),
            shaped((slots, units), bf16),
            shaped((units, features), bf16),
        ],
        cost_estimate=pl.CostEstimate(
            flops=4 * slots * features * units, bytes_accessed=30 << 20, transcendentals=0
        ),
        name="expert_forward",
    )(*xs, *gs, up, up_bias)


def accumulate(acc_ref, value, initial=None):
    @pl.when(pl.program_id(0) == 0)
    def _():
        acc_ref[...] = value if initial is None else value + initial

    @pl.when(pl.program_id(0) > 0)
    def _():
        acc_ref[...] += value


def emit_chunks(acc_ref, outs):
    @pl.when(pl.program_id(0) == pl.num_programs(0) - 1)
    def _():
        stride = acc_ref.shape[0] // len(outs)
        for d, out in enumerate(outs):
            out[...] = acc_ref[d * stride : (d + 1) * stride, :].astype(bf16)


def expert_out_kernel(count, hid_ref, down_ref, bias_ref, *refs):
    outs, acc_ref = refs[:count], refs[count]
    accumulate(acc_ref, dot(hid_ref[...], down_ref[...], NN), bias_ref[...])
    emit_chunks(acc_ref, outs)


def expert_out(hidden, down, bias, count, tile=768):
    slots, units = hidden.shape
    features = down.shape[1]
    return pl.pallas_call(
        functools.partial(expert_out_kernel, count),
        grid=(units // tile,),
        in_specs=[
            pl.BlockSpec((slots, tile), lambda j: (0, j)),
            pl.BlockSpec((tile, features), lambda j: (j, 0)),
            full((1, features)),
        ],
        out_specs=[full((slots // count, features))] * count,
        out_shape=[shaped((slots // count, features), bf16)] * count,
        scratch_shapes=[pltpu.VMEM((slots, features), f32)],
        cost_estimate=pl.CostEstimate(
            flops=2 * slots * features * units, bytes_accessed=12 << 20, transcendentals=0
        ),
        name="expert_out",
    )(hidden, down, bias)


def expert_back_kernel(count, sg_ref, down_ref, pre_ref, up_ref, inner_ref, sums_ref, *refs):
    outs, acc_ref = refs[:count], refs[count]
    slots, block = acc_ref.shape[0], 256
    total = jnp.zeros(sums_ref.shape, f32)
    for m in range(0, slots, block):
        rows = slice(m, m + block)
        slope = gelu_slope(pre_ref[rows, :].astype(f32))
        low = (dot(sg_ref[rows, :], down_ref[...], NT) * slope).astype(bf16)
        inner_ref[rows, :] = low
        total += jnp.sum(low.astype(f32), axis=0, keepdims=True)
    sums_ref[...] = total
    accumulate(acc_ref, dot(inner_ref[...], up_ref[...], NT))
    emit_chunks(acc_ref, outs)


def expert_back(slot_grad, down, pre, up, count, tile=768):
    slots, features = slot_grad.shape
    units = up.shape[1]
    return pl.pallas_call(
        functools.partial(expert_back_kernel, count),
        grid=(units // tile,),
        in_specs=[
            full((slots, features)),
            pl.BlockSpec((tile, features), lambda j: (j, 0)),
            pl.BlockSpec((slots, tile), lambda j: (0, j)),
            pl.BlockSpec((features, tile), lambda j: (0, j)),
        ],
        out_specs=[
            pl.BlockSpec((slots, tile), lambda j: (0, j)),
            pl.BlockSpec((1, tile), lambda j: (0, j)),
        ]
        + [full((slots // count, features))] * count,
        out_shape=[shaped((slots, units), bf16), shaped((1, units), f32)]
        + [shaped((slots // count, features), bf16)] * count,
        scratch_shapes=[pltpu.VMEM((slots, features), f32)],
        cost_estimate=pl.CostEstimate(
            flops=4 * slots * features * units, bytes_accessed=24 << 20, transcendentals=0
        ),
        name="expert_back",
    )(slot_grad, down, pre, up)


def up_gradient_kernel(x_ref, inner_ref, out_ref):
    block = 256
    for n in range(0, x_ref.shape[1], block):
        cols = slice(n, n + block)
        out_ref[cols, :] = dot(x_ref[:, cols], inner_ref[...], TN).astype(bf16)


def up_gradient(x, inner, tile=768):
    slots, features = x.shape
    units = inner.shape[1]
    return pl.pallas_call(
        up_gradient_kernel,
        grid=(units // tile,),
        in_specs=[full((slots, features)), pl.BlockSpec((slots, tile), lambda j: (0, j))],
        out_specs=pl.BlockSpec((features, tile), lambda j: (0, j)),
        out_shape=shaped((features, units), bf16),
        cost_estimate=pl.CostEstimate(
            flops=2 * slots * features * units, bytes_accessed=12 << 20, transcendentals=0
        ),
        name="up_gradient",
    )(x, inner)


def combine_kernel(experts, stride, *refs):
    chunks = refs[:experts]
    flat_ref, ids_ref, gate_ref, residual_ref, grad_ref, out_ref, logit_ref = refs[experts:-1]
    rows_ref = refs[-1]
    for d in range(experts):
        rows_ref[d * stride : (d + 1) * stride, :] = chunks[d][...]
    slots = experts * stride
    slot = lax.broadcasted_iota(jnp.int32, (1, slots), 1)
    gates = gate_ref[...]
    grads = grad_ref[...].astype(f32)
    total = residual_ref[...]
    mass = jnp.zeros_like(gates)
    for k in range(2):
        hits = (flat_ref[:, k : k + 1] == slot).astype(f32).astype(bf16)
        picked = dot(hits, rows_ref[...], NN)
        choice = choice_of(ids_ref, k)
        total += jnp.sum(jnp.where(choice, gates, 0.0), axis=1, keepdims=True) * picked
        gate_grad = jnp.sum(grads * picked, axis=1, keepdims=True)
        mass += jnp.where(choice, gate_grad, 0.0)
    out_ref[...] = total.astype(bf16)
    logit_ref[...] = (gates * (mass - jnp.sum(gates * mass, axis=1, keepdims=True))).astype(bf16)


def combine(chunks, flat, ids, gates, residual, grad_low):
    experts, (stride, features) = len(chunks), chunks[0].shape
    tokens = residual.shape[0]
    return pl.pallas_call(
        functools.partial(combine_kernel, experts, stride),
        out_shape=[shaped((tokens, features), bf16), shaped((tokens, LANES), bf16)],
        scratch_shapes=[pltpu.VMEM((experts * stride, features), bf16)],
        cost_estimate=pl.CostEstimate(
            flops=4 * tokens * experts * stride * features, bytes_accessed=6 << 20, transcendentals=0
        ),
        name="combine",
    )(*chunks, flat, ids, gates, residual, grad_low)


def split_rows(value_ref, offsets_ref, width, kept_ref, sent_ref):
    blocks = 2 * kept_ref.shape[0]
    rows = kept_ref.shape[1]
    for d in range(blocks):
        part = value_ref[pl.ds(pl.multiple_of(offsets_ref[d], 8), rows), :].astype(bf16)
        (kept_ref, sent_ref)[d % 2][d // 2, :, width] = part


def residual_back_kernel(experts, stride, offsets_ref, *refs):
    chunks = refs[:experts]
    (
        flat_ref,
        logit_ref,
        router_ref,
        two_ref,
        residual_ref,
        grad_ref,
        par_ref,
        w_ref,
        att_ref,
        residual_grad_ref,
        att_grad_ref,
        kept_ref,
        sent_ref,
        rows_ref,
        vector_ref,
        value_ref,
        small_ref,
    ) = refs[experts:]
    for d in range(experts):
        rows_ref[d * stride : (d + 1) * stride, :] = chunks[d][...]
    features = residual_ref.shape[1]
    slot = lax.broadcasted_iota(jnp.int32, (1, experts * stride), 1)
    hits = (flat_ref[:, 0:1] == slot) | (flat_ref[:, 1:2] == slot)
    two_grad = dot(hits.astype(f32).astype(bf16), rows_ref[...], NN)
    two_grad += dot(logit_ref[...], router_ref[...], NT)
    hat, scale = normalise(residual_ref[...])
    residual_grad = grad_ref[...].astype(f32) + normalise_back(two_grad, hat, scale, par_ref[1:2])
    residual_grad_ref[...] = residual_grad
    branch = residual_grad.astype(bf16)
    vector_ref[...] = jnp.zeros_like(vector_ref)
    vector_ref[0:1] = jnp.sum(two_grad * hat, axis=0, keepdims=True)
    vector_ref[1:2] = jnp.sum(two_grad, axis=0, keepdims=True)
    vector_ref[2:3] = jnp.sum(residual_grad, axis=0, keepdims=True)
    att_grad_ref[...] = dot(branch, w_ref[...], NT).astype(bf16)
    value_ref[...] = dot(att_ref[...], branch, TN)
    split_rows(value_ref, offsets_ref, slice(0, features), kept_ref, sent_ref)
    small_ref[...] = dot(two_ref[...], logit_ref[...], TN)
    split_rows(small_ref, offsets_ref, slice(features, features + LANES), kept_ref, sent_ref)
    small_ref[...] = jnp.transpose(vector_ref[...])
    split_rows(
        small_ref, offsets_ref, slice(features + LANES, features + 2 * LANES), kept_ref, sent_ref
    )


def residual_back(
    chunks, flat, logit_grad, first_full, two, residual, grad_low, par, w, att, offsets
):
    experts, (stride, features) = len(chunks), chunks[0].shape
    tokens = residual.shape[0]
    column = first_full.shape[1] // LANES - 1
    size = offsets.shape[0]
    packed = (size // 2, features // size, features + 2 * LANES)
    return pl.pallas_call(
        functools.partial(residual_back_kernel, experts, stride),
        grid_spec=pltpu.PrefetchScalarGridSpec(
            num_scalar_prefetch=1,
            grid=(1,),
            in_specs=[full((stride, features))] * experts
            + [
                full(flat.shape),
                full(logit_grad.shape),
                pl.BlockSpec((features, LANES), lambda i, o: (0, column)),
            ]
            + [full(value.shape) for value in (two, residual, grad_low, par, w, att)],
            out_specs=[full((tokens, features))] * 2 + [full(packed)] * 2,
            scratch_shapes=[
                pltpu.VMEM((experts * stride, features), bf16),
                pltpu.VMEM((LANES, features), f32),
                pltpu.VMEM((features, features), f32),
                pltpu.VMEM((features, LANES), f32),
            ],
        ),
        out_shape=[
            shaped((tokens, features), f32),
            shaped((tokens, features), bf16),
            shaped(packed, bf16),
            shaped(packed, bf16),
        ],
        cost_estimate=pl.CostEstimate(
            flops=8 * tokens * features * features, bytes_accessed=10 << 20, transcendentals=0
        ),
        name="residual_back",
    )(
        offsets, *chunks, flat, logit_grad, first_full, two, residual, grad_low, par, w, att
    )


def attend_back_kernel(proj_ref, prob_ref, out_grad_ref, grad_ref):
    features = out_grad_ref.shape[1]
    low = lax.broadcasted_iota(jnp.int32, (1, LANES), 1) < HEAD_DIM

    def pair(p, carry):
        def cols(third):
            return pl.ds(pl.multiple_of(third * features + p * LANES, LANES), LANES)

        query, key, value = (proj_ref[:, cols(third)] for third in range(3))
        grads = out_grad_ref[:, cols(0)]
        results = []
        for half in range(2):
            mine = low if half == 0 else ~low
            low_probs = prob_ref[2 * p + half]
            probs = low_probs.astype(f32)
            weight_grad = dot(jnp.where(mine, grads, jnp.zeros_like(grads)), value, NT)
            total = jnp.sum(weight_grad * probs, axis=1, keepdims=True)
            score_grad = (probs * (weight_grad - total)).astype(bf16)
            results.append(
                (
                    dot(score_grad, key, NN) * HEAD_DIM**-0.5,
                    dot(score_grad, query, TN) * HEAD_DIM**-0.5,
                    dot(low_probs, grads, TN),
                )
            )
        for third in range(3):
            grad_ref[:, cols(third)] = jnp.where(
                low, results[0][third], results[1][third]
            ).astype(bf16)
        return carry

    lax.fori_loop(0, features // LANES, pair, 0, unroll=3)


def attend_back(proj, probs, out_grad, images):
    tokens, features = out_grad.shape
    padded = tokens // images
    image = lambda i: (i, 0)
    return pl.pallas_call(
        attend_back_kernel,
        grid=(images,),
        in_specs=[
            pl.BlockSpec((padded, 3 * features), image),
            pl.BlockSpec((HEADS, padded, padded), lambda i: (i, 0, 0)),
            pl.BlockSpec((padded, features), image),
        ],
        out_specs=pl.BlockSpec((padded, 3 * features), image),
        out_shape=shaped((tokens, 3 * features), bf16),
        cost_estimate=pl.CostEstimate(
            flops=12 * tokens * features * features, bytes_accessed=6 << 20, transcendentals=0
        ),
        name="attend_back",
    )(proj, probs, out_grad)


def input_back_kernel(
    offsets_ref,
    norm_ref,
    grad_ref,
    w_ref,
    x_ref,
    residual_grad_ref,
    par_ref,
    out_ref,
    kept_ref,
    sent_ref,
    acc_ref,
    vector_ref,
    value_ref,
    small_ref,
):
    features = x_ref.shape[1]
    vector_ref[...] = jnp.zeros_like(vector_ref)
    for third in range(3):
        cols = slice(third * features, (third + 1) * features)
        value_ref[...] = dot(norm_ref[...], grad_ref[:, cols], TN)
        split_rows(value_ref, offsets_ref, cols, kept_ref, sent_ref)
        value = dot(grad_ref[:, cols], w_ref[:, cols], NT)
        if third == 0:
            acc_ref[...] = value
        else:
            acc_ref[...] += value
        if third != 1:
            row = 2 + third // 2
            vector_ref[row : row + 1] = jnp.sum(
                grad_ref[:, cols].astype(f32), axis=0, keepdims=True
            )
    hat, scale = normalise(x_ref[...].astype(f32))
    grads = acc_ref[...]
    vector_ref[0:1] = jnp.sum(grads * hat, axis=0, keepdims=True)
    vector_ref[1:2] = jnp.sum(grads, axis=0, keepdims=True)
    small_ref[...] = jnp.transpose(vector_ref[...])
    split_rows(
        small_ref, offsets_ref, slice(3 * features, 3 * features + LANES), kept_ref, sent_ref
    )
    out_ref[...] = (
        residual_grad_ref[...] + normalise_back(grads, hat, scale, par_ref[0:1])
    ).astype(bf16)


def input_back(norm, grads, first_full, x, residual_grad, par, offsets):
    tokens, features = x.shape
    size = offsets.shape[0]
    packed = (size // 2, features // size, 3 * features + LANES)
    return pl.pallas_call(
        input_back_kernel,
        grid_spec=pltpu.PrefetchScalarGridSpec(
            num_scalar_prefetch=1,
            grid=(1,),
            in_specs=[full(norm.shape), full(grads.shape), full((features, 3 * features))]
            + [full(value.shape) for value in (x, residual_grad, par)],
            out_specs=[full((tokens, features))] + [full(packed)] * 2,
            scratch_shapes=[
                pltpu.VMEM((tokens, features), f32),
                pltpu.VMEM((LANES, features), f32),
                pltpu.VMEM((features, features), f32),
                pltpu.VMEM((features, LANES), f32),
            ],
        ),
        out_shape=[shaped((tokens, features), bf16), shaped(packed, bf16), shaped(packed, bf16)],
        cost_estimate=pl.CostEstimate(
            flops=12 * tokens * features * features, bytes_accessed=16 << 20, transcendentals=0
        ),
        name="input_back",
    )(offsets, norm, grads, first_full, x, residual_grad, par)


def finish_kernel(parts, offsets_ref, *refs):
    pieces, (joint_ref, out_ref, rest_ref) = refs[:parts], refs[parts:]
    joint, features = joint_ref.shape[1], out_ref.shape[1]
    for k, piece in enumerate(pieces):
        value = piece[...].astype(f32)
        rows = pl.ds(pl.multiple_of(offsets_ref[k], 8), value.shape[0])
        joint_ref[rows, :] = value[:, :joint]
        rest_ref[rows, :LANES] = value[:, joint : joint + LANES]
        out_ref[rows, :] = value[:, joint + LANES : joint + LANES + features]
        rest_ref[rows, LANES:] = value[:, joint + LANES + features :]


def finish(pieces, offsets, rows, features):
    return pl.pallas_call(
        functools.partial(finish_kernel, len(pieces)),
        grid_spec=pltpu.PrefetchScalarGridSpec(
            num_scalar_prefetch=1,
            grid=(1,),
            in_specs=[full(piece.shape) for piece in pieces],
            out_specs=[full((rows, width)) for width in (3 * features, features, 3 * LANES)],
        ),
        out_shape=[shaped((rows, width), f32) for width in (3 * features, features, 3 * LANES)],
        name="finish",
    )(offsets, *pieces)


def plane_sums(kept, sent, expert_size):
    partner = swap(sent, "expert", expert_size, 1)
    pair_sum = (kept.astype(f32) + partner.astype(f32)).astype(bf16)
    parts = [swap(pair_sum[d // 2], "expert", expert_size, d) for d in range(2, expert_size, 2)]
    return sum((part.astype(f32) for part in parts), pair_sum[0].astype(f32)).astype(bf16)


def dp_sums(plane_sum, dp_size, dp_index, features):
    rows = plane_sum.shape[0]
    plane_sum = plane_sum.reshape(dp_size, rows // dp_size, -1)
    dp_parts = exchange(
        [
            lax.dynamic_index_in_dim(plane_sum, dp_index ^ d, 0, keepdims=False)
            for d in range(dp_size)
        ],
        "dp",
        dp_size,
    )
    dp_sum = sum(part.astype(f32) for part in dp_parts).astype(bf16)
    whole = lax.all_gather(dp_sum, "dp", axis=0, tiled=True)
    return finish([whole], jnp.zeros((1,), jnp.int32), rows, features)


def per_device(
    block_input,
    out_grad,
    expert_ids,
    slot_order,
    joint_weight,
    out_weight,
    router_weight,
    norm_gains,
    norm_shifts,
    attention_bias,
    up_weight,
    down_weight,
    up_bias,
    down_bias,
    *,
    expert_size,
    dp_size,
):
    index = lax.axis_index("expert")
    dp_index = lax.axis_index("dp")
    row_count, features = block_input.shape
    images = row_count // SEQ
    experts = router_weight.shape[1]
    capacity = max(2, (5 * row_count + 2 * experts - 1) // (2 * experts))
    stride = round_up(capacity + 1, 16)
    slots = experts * stride
    padded = round_up(SEQ, 16)
    tokens = images * padded
    hidden_units = up_weight.shape[2]
    block_rows = features // expert_size
    row_offsets = (index ^ jnp.arange(expert_size, dtype=jnp.int32)) * block_rows

    def pad_rows(values, fill=0):
        split = values.reshape(images, SEQ, values.shape[-1])
        return jnp.pad(
            split, ((0, 0), (0, padded - SEQ), (0, 0)), constant_values=fill
        ).reshape(tokens, values.shape[-1])

    def crop_rows(values):
        return values.reshape(images, padded, -1)[:, :SEQ].reshape(row_count, -1)

    small = jnp.concatenate(
        [router_weight, norm_gains.T, norm_shifts.T, attention_bias.T], axis=1
    )
    small = jnp.pad(small, ((0, 0), (0, LANES - small.shape[1])))
    first, first_offsets = gather_pieces(
        jnp.concatenate([joint_weight, small], axis=1), "expert", expert_size
    )
    input_low, grad_low = pad_rows(block_input), pad_rows(out_grad)
    ids = pad_rows(expert_ids)
    flat = pad_rows(
        slot_index(expert_ids, slot_order[0], experts, capacity, stride, index), slots
    )
    grad_slots = scatter_rows(flat, grad_low, experts, stride)
    second, second_offsets = gather_pieces(out_weight, "expert", expert_size)
    first, grad_slots, ids, input_low = lax.optimization_barrier(
        (first, grad_slots, ids, input_low)
    )
    grad_arrived = exchange(grad_slots, "expert", expert_size)

    first_full, par, normed, projected, probs, attended = attend(
        input_low, first, first_offsets, experts, images
    )
    out_full, residual, two_low, gates, *dispatched = middle(
        attended,
        input_low,
        first_full,
        par,
        flat,
        ids,
        second,
        second_offsets,
        experts,
        stride,
        capacity,
    )
    arrived = exchange(dispatched, "expert", expert_size)

    up, down = up_weight[0], down_weight[0]
    rows, slot_grad, hidden, pre, down_local = expert_forward(
        arrived, grad_arrived, up, up_bias.astype(f32), capacity
    )
    down_part = lax.psum_scatter(down_local, "dp", scatter_dimension=0, tiled=True)
    expert_low = expert_out(hidden, down, down_bias.astype(f32), experts)
    returned = exchange(expert_low, "expert", expert_size)
    inner, inner_sums, *rows_grad = expert_back(slot_grad, down, pre, up, experts)
    rows_back = exchange(rows_grad, "expert", expert_size)
    up_local = up_gradient(rows, inner)
    up_part = lax.psum_scatter(up_local, "dp", scatter_dimension=1, tiled=True)
    bias_local = jnp.concatenate(
        [
            inner_sums.reshape(dp_size, -1),
            jnp.sum(slot_grad, axis=0, dtype=f32).reshape(dp_size, -1),
        ],
        axis=1,
    )
    bias_chunks = [
        lax.dynamic_index_in_dim(bias_local, dp_index ^ d, 0) for d in range(dp_size)
    ]
    bias_sum = sum(exchange(bias_chunks, "dp", dp_size))
    up_bias_grad = bias_sum[:, : hidden_units // dp_size]
    down_bias_grad = bias_sum[:, hidden_units // dp_size :]

    block_output, logit_grad = combine(returned, flat, ids, gates, residual, grad_low)
    residual_grad, attended_grad, kept, sent = residual_back(
        rows_back,
        flat,
        logit_grad,
        first_full,
        two_low,
        residual,
        grad_low,
        par,
        out_full,
        attended,
        row_offsets,
    )
    late = plane_sums(kept, sent, expert_size)
    projected_grad = attend_back(projected, probs, attended_grad, images)
    input_grad, kept, sent = input_back(
        normed, projected_grad, first_full, input_low, residual_grad, par, row_offsets
    )
    early = plane_sums(kept, sent, expert_size)
    early, down_part = lax.optimization_barrier((early, down_part.astype(f32)))
    joint_grad, out_weight_grad, rest = dp_sums(
        jnp.concatenate([early, late], axis=1), dp_size, dp_index, features
    )
    early_vectors = rest[:, :4].T
    late_vectors = rest[:, 2 * LANES : 2 * LANES + 3].T
    return (
        crop_rows(block_output),
        crop_rows(input_grad),
        joint_grad,
        out_weight_grad,
        rest[:, LANES : LANES + experts],
        jnp.stack([early_vectors[0], late_vectors[0]]),
        jnp.stack([early_vectors[1], late_vectors[1]]),
        jnp.stack([early_vectors[2], early_vectors[3], late_vectors[2]]),
        up_part[None].astype(f32),
        down_part[None],
        up_bias_grad,
        down_bias_grad,
    )


def solution(mesh):
    def body(*args):
        return per_device(
            *args, expert_size=mesh.shape["expert"], dp_size=mesh.shape["dp"]
        )

    in_specs = (
        P(("dp", "expert"), None),
        P(("dp", "expert"), None),
        P(("dp", "expert"), None),
        P(("dp", "expert"), None),
        P("expert", None),
        P("expert", None),
        P("expert", None),
        P(None, "expert"),
        P(None, "expert"),
        P(None, "expert"),
        P("expert", None, None),
        P("expert", None, None),
        P("expert", None),
        P("expert", None),
    )
    out_specs = (
        P(("dp", "expert"), None),
        P(("dp", "expert"), None),
        P("expert", None),
        P("expert", None),
        P("expert", None),
        P(None, "expert"),
        P(None, "expert"),
        P(None, "expert"),
        P("expert", None, "dp"),
        P("expert", "dp", None),
        P("expert", "dp"),
        P("expert", "dp"),
    )
    return jax.shard_map(
        body, mesh=mesh, in_specs=in_specs, out_specs=out_specs, check_vma=False
    )
```
